256 devices in a mesh: gx: 8 (over y, core), gy: 4 (over x), gz: 8 (over z).
Axes of the slice: x: 4, y: 4, z: 8, core: 2. Of those that a mesh axis runs over, the one named last changes fastest.
Arguments:
- old_fields: float32 [16384, 4, 512], P(('gx', 'gy', 'gz')), may hold values from 0.5 to 2.5
- new_owner: int32 [16384], P(('gx', 'gy', 'gz')), may hold values from 0 to 63, as said below
- old_owner: int32 [16384], P(('gx', 'gy', 'gz')), may hold values from 0 to 63, as said below
Outputs:
- flame_fields: float32 [4, 128, 64, 1024], P(None, 'gx', 'gy', 'gz')
The draws below stay inside these ranges and needn't reach their ends.
Inputs may be any that keep to these rules, and one draw needn't show every extreme that they name: A box keeps its gy index; new_owner is the group index of the device of its gx+gz group that holds it after the move. A device sends at most 2 boxes to one device of its group, reaches that number for some device, and every device receives exactly 64 boxes. `old_owner`: agrees with new_owner: the positions of a device naming s are exactly as many as the boxes that device s of the same group and gy sends to it.
All inputs are finite; a program needn't handle non-finite values.
Results may differ from the reference program's by a relative error of at most 0.00002.
Values sent between devices are 32-bit elements; how exact they have to be, the bound alone decides.
A program may use at most 64 MiB of HBM per device.

```python
import jax
import jax.numpy as jnp

EDGE = 8
FIELDS = 4
BRICK_X = 2
BRICK_Y = 2
BRICK_Z = 16
BOX_DEV = 64
CELLS = 512
NBOXES = 16384
NX = 128
NY = 64
NZ = 1024
N_GX = 8
N_GY = 4
N_GZ = 8


def routing(key):
    group_size = N_GX * N_GZ
    share_count = BOX_DEV // group_size
    base_key = jax.random.fold_in(key, 7)

    def one_plane(slab_key):
        plane_keys = jax.random.split(slab_key, 4)
        mapping = jax.random.permutation(plane_keys[0], group_size)
        offsets = jax.random.randint(plane_keys[1], (share_count,), 1, group_size)
        sources = jnp.arange(group_size, dtype=jnp.int32)
        targets = jnp.arange(group_size, dtype=jnp.int32)
        counts = share_count + share_count * (mapping[:, None] == targets[None, :]).astype(jnp.int32)
        shifted = mapping[(sources[None, :] + offsets[:, None]) % group_size]
        counts = counts - jnp.sum((shifted[:, :, None] == targets[None, None, :]).astype(jnp.int32), axis=0)

        def one_source(row_counts, row_key):
            listed = jnp.repeat(targets, row_counts, total_repeat_length=BOX_DEV)
            return jax.random.permutation(row_key, listed)

        def one_target(column_counts, column_key):
            listed = jnp.repeat(sources, column_counts, total_repeat_length=BOX_DEV)
            return jax.random.permutation(column_key, listed)
        sent_to = jax.vmap(one_source)(counts, jax.random.split(plane_keys[2], group_size))
        held_from = jax.vmap(one_target)(counts.T, jax.random.split(plane_keys[3], group_size))
        return (sent_to, held_from)
    sent_to, held_from = jax.vmap(one_plane)(jax.random.split(base_key, N_GY))
    sent_to = sent_to.reshape(N_GY, N_GX, N_GZ, BOX_DEV).transpose(1, 0, 2, 3).reshape(-1)
    held_from = held_from.reshape(N_GY, N_GX, N_GZ, BOX_DEV).transpose(1, 0, 2, 3).reshape(-1)
    return (sent_to.astype(jnp.int32), held_from.astype(jnp.int32))


def draw_new_owner(key, part):
    return routing(key)[0]


def draw_old_owner(key, part):
    return routing(key)[1]


def shard_levels(key, shape, cuts, least, high):
    gain = 1.0
    for dim, shards_of in cuts:
        draws = jax.random.uniform(jax.random.fold_in(jax.random.fold_in(key, 6), dim), (shards_of,), jnp.float32, least / len(cuts), high / len(cuts))
        gain = gain * jnp.repeat(jnp.exp(draws), shape[dim] // shards_of).reshape((-1,) + (1,) * (len(shape) - 1 - dim))
    return gain


def setup_inputs(seed: int = 0) -> dict:
    seeds = jax.random.split(jax.random.key(seed), 4)
    return {
        "old_fields": jnp.clip(0.5 + 2.0 * jax.random.uniform(seeds[0], (NBOXES, FIELDS, CELLS), jnp.float32) ** shard_levels(seeds[0], (NBOXES, FIELDS, CELLS), ((0, 256),), -0.2, 0.2), 0.5, 2.5),
        "new_owner": draw_new_owner(jax.random.fold_in(seeds[3], 71), 0),
        "old_owner": draw_old_owner(jax.random.fold_in(seeds[3], 71), 0),
    }


DIFFUSION = (1.0, 3.3, 0.9, 1.2)
TIME_STEP = 0.012

def diffusion_rate(present_state):
    thermal_field = present_state[0]
    stepping_factors = jnp.array(DIFFUSION, jnp.float32)
    diffusion_coefficient = stepping_factors[:, None, None, None] * (thermal_field * jnp.sqrt(thermal_field))[None]
    summed = jnp.zeros_like(present_state)
    for direction in (1, 2, 3):
        for offset in (1, -1):
            beside = jnp.roll(present_state, offset, axis=direction)
            beside_diffusivity = jnp.roll(diffusion_coefficient, offset, axis=direction)
            summed = summed + 0.5 * (diffusion_coefficient + beside_diffusivity) * (beside - present_state)
    return summed

def reference(old_fields, new_owner, old_owner):
    group_size = N_GX * N_GZ
    row_number = jnp.arange(NBOXES, dtype=jnp.int32)
    device = row_number // BOX_DEV
    slot_number = row_number % BOX_DEV
    plane_index = device // N_GZ % N_GY
    source_group = device // (N_GY * N_GZ) * N_GZ + device % N_GZ
    target_device = (new_owner // N_GZ * N_GY + plane_index) * N_GZ + new_owner % N_GZ
    old_keys = (target_device * group_size + source_group) * BOX_DEV + slot_number
    new_keys = (device * group_size + old_owner) * BOX_DEV + slot_number
    old_order = jnp.argsort(old_keys).astype(jnp.int32)
    new_order = jnp.argsort(new_keys).astype(jnp.int32)
    sources = jnp.zeros((NBOXES,), jnp.int32).at[new_order].set(old_order)
    moved_boxes = jnp.take(old_fields, sources, axis=0)
    present_state = moved_boxes.reshape(N_GX, N_GY, N_GZ, BRICK_X, BRICK_Y, BRICK_Z, FIELDS, EDGE, EDGE, EDGE)
    present_state = present_state.transpose(6, 0, 3, 7, 1, 4, 8, 2, 5, 9).reshape(FIELDS, NX, NY, NZ)
    first_section = present_state + TIME_STEP * diffusion_rate(present_state)
    return 0.5 * present_state + 0.5 * (first_section + TIME_STEP * diffusion_rate(first_section))
```

```python
import jax
import jax.numpy as jnp
from jax import lax
from jax.experimental import pallas as pl
from jax.experimental.pallas import tpu as pltpu
from jax.sharding import PartitionSpec as P

DIFFUSION = (1.0, 3.3, 0.9, 1.2)
TIME_STEP = 0.012
MESH = pl.DeviceIdType.MESH
F = 4
PLANE = 16
PAIR = F * 2 * PLANE


def row_of(x, f):
    x = x + 2
    return pl.multiple_of((x // 2) * PAIR + f * 2 * PLANE + (x % 2) * PLANE, PLANE)


def coefficient(t):
    return t * jnp.sqrt(t)


def kernel(
    old_hbm, new_owner, old_owner, out,
    old, send, recv, grid0, grid1, diff, fx, fy, fz, hx, hy, hz, index_v, index_s,
    old_sem, index_sem, send_sem, recv_sem, face_send, face_recv,
):
    gx, gy, gz = lax.axis_index("gx"), lax.axis_index("gy"), lax.axis_index("gz")
    load = pltpu.make_async_copy(old_hbm, old, old_sem)
    load.start()

    barrier = pltpu.get_barrier_semaphore()
    up_y, down_y = (gy + 1) % 4, (gy + 3) % 4
    for y in (up_y, down_y):
        pl.semaphore_signal(barrier, inc=1, device_id={"gy": y}, device_id_type=MESH)

    def peer(r):
        return (gx + r // 8) % 8, (gz + r % 8) % 8

    def greet(r, c):
        px, pz = peer(r)
        pl.semaphore_signal(barrier, inc=1, device_id={"gx": px, "gz": pz}, device_id_type=MESH)
        return c

    lax.fori_loop(1, 64, greet, 0)

    lane = lax.broadcasted_iota(jnp.int32, (8, 128), 1)

    def leaving(i, c):
        first, last = c
        hit = lane == new_owner[i]
        return jnp.where(hit & (first < 0), i, first), jnp.where(hit, i, last)

    none = jnp.full((8, 128), -1, jnp.int32)
    first, last = lax.fori_loop(0, 64, leaving, (none, none))
    index_v[0] = jnp.maximum(first, 0)
    index_v[1] = jnp.maximum(last, 0)
    to_s = pltpu.make_async_copy(index_v.at[pl.ds(0, 2)], index_s.at[pl.ds(0, 2)], index_sem.at[0])
    to_s.start()
    load.wait()
    to_s.wait()

    def pack(r, c):
        px, pz = peer(r)
        owner = px * 8 + pz
        send[2 * r] = old[index_s[0, 0, owner]]
        send[2 * r + 1] = old[index_s[1, 0, owner]]
        return c

    lax.fori_loop(0, 64, pack, 0)
    recv[0] = send[0]
    recv[1] = send[1]
    pl.semaphore_wait(barrier, 65)

    def post(r, c):
        px, pz = peer(r)
        slot = ((8 - r // 8) % 8) * 8 + (8 - r % 8) % 8
        pltpu.make_async_remote_copy(
            src_ref=send.at[pl.ds(2 * r, 2)],
            dst_ref=recv.at[pl.ds(2 * slot, 2)],
            send_sem=send_sem,
            recv_sem=recv_sem,
            device_id={"gx": px, "gz": pz},
            device_id_type=MESH,
        ).start()
        return c

    lax.fori_loop(1, 64, post, 0)

    def owners(i, c):
        return jnp.where(lane == i, old_owner[i], c)

    owner = lax.fori_loop(0, 64, owners, none)

    def ranks(i, c):
        return jnp.where((lane > i) & (owner == old_owner[i]), 1, c)

    rank = lax.fori_loop(0, 64, ranks, jnp.zeros((8, 128), jnp.int32))
    slot = ((owner // 8 - gx + 8) % 8) * 8 + (owner % 8 - gz + 8) % 8
    index_v[2] = slot * 2 + rank
    to_s = pltpu.make_async_copy(index_v.at[pl.ds(2, 1)], index_s.at[pl.ds(2, 1)], index_sem.at[1])
    to_s.start()
    to_s.wait()

    everyone = recv.at[pl.ds(2, 126)]
    pltpu.make_async_copy(everyone, everyone, recv_sem).wait()

    def reorder(s, c):
        bx, by, h = s // 4, (s // 2) % 2, s % 2
        v = [recv[index_s[2, 0, (bx * 2 + by) * 16 + bz], h] for bz in range(16)]
        for step in (1, 2, 4, 8):
            low = ((lane // 8) & step) == 0
            for a in range(16):
                if not a & step:
                    b = a + step
                    v[a], v[b] = (
                        jnp.where(low, v[a], pltpu.roll(v[b], 8 * step, 1)),
                        jnp.where(low, pltpu.roll(v[a], 128 - 8 * step, 1), v[b]),
                    )
        for g in range(16):
            start = (bx * 4 + h * 2 + 1) * PAIR + (g // 8) * PLANE + by * 8 + g % 8
            grid0[pl.ds(start, 8, stride=2 * PLANE), :] = v[g]
        return c

    lax.fori_loop(0, 8, reorder, 0)

    def pack_z(x, f, half, value, ends):
        m = x * 8 + f * 2 + half
        here = lane == m
        return (
            jnp.where(here, pltpu.roll(value, m, 1), ends[0]),
            jnp.where(here, pltpu.roll(value, (m + 1) % 128, 1), ends[1]),
        )

    def exchange(k, grid, ends):
        for side, x in ((0, 0), (1, 15)):
            for f in range(F):
                fx[k, side, pl.ds(f * 16, 16)] = grid[pl.ds(row_of(x, f), 16), :]
        for side, y in ((0, 0), (1, 15)):
            for f in range(F):
                for odd in range(2):
                    fy[k, side, pl.ds((f * 2 + odd) * 8, 8)] = grid[
                        pl.ds(PAIR + (f * 2 + odd) * 16 + y, 8, stride=PAIR), :
                    ]
        for side in range(2):
            fz[k, side] = ends[side]
        copies = []
        for n, (faces, halos, axis, here, size) in enumerate(
            ((fz, hz, "gz", gz, 8), (fy, hy, "gy", gy, 4), (fx, hx, "gx", gx, 8))
        ):
            for side in range(2):
                there = (here + (1 if side else size - 1)) % size
                copy = pltpu.make_async_remote_copy(
                    src_ref=faces.at[k, side],
                    dst_ref=halos.at[k, 1 - side],
                    send_sem=face_send.at[k, n, side],
                    recv_sem=face_recv.at[k, n, 1 - side],
                    device_id={axis: there},
                    device_id_type=MESH,
                )
                copy.start()
                copies.append((copy, n, side))
        for copy, _, _ in copies:
            copy.wait()
        for side, x in ((0, -1), (1, 16)):
            for f in range(F):
                grid[pl.ds(row_of(x, f), 16), :] = hx[k, side, pl.ds(f * 16, 16)]

    sub = lax.broadcasted_iota(jnp.int32, (16, 128), 0)
    wide = lax.broadcasted_iota(jnp.int32, (16, 128), 1)

    def section(k, grid, emit, start):
        def diffusivity(x, c):
            diff[pl.ds(pl.multiple_of(x * 16, 16), 16), :] = coefficient(grid[pl.ds(row_of(x - 1, 0), 16), :])
            return c

        lax.fori_loop(0, 18, diffusivity, 0)
        z_low, z_high = hz[k, 0], hz[k, 1]
        z_low_d, z_high_d = coefficient(z_low), coefficient(z_high)

        def ends_of(low, high, x, f):
            m = x * 8 + f * 2
            return (
                jnp.concatenate([pltpu.roll(low, (128 - m - h) % 128, 1) for h in range(2)], 0),
                jnp.concatenate([pltpu.roll(high, 127 - m - h, 1) for h in range(2)], 0),
            )

        def around(v, low_row, high_row, low_z, high_z):
            return (
                jnp.where(sub == 0, low_row, pltpu.roll(v, 1, 0)),
                jnp.where(sub == 15, high_row, pltpu.roll(v, 15, 0)),
                jnp.where(wide == 0, low_z, pltpu.roll(v, 1, 1)),
                jnp.where(wide == 127, high_z, pltpu.roll(v, 127, 1)),
            )

        def edge_row(side, x, f):
            return hy[k, side, pl.ds((f * 2 + x % 2) * 8 + x // 2, 1), :]

        def plane(x, c):
            d = [diff[pl.ds(pl.multiple_of((x + n) * 16, 16), 16), :] for n in range(3)]
            low_z, high_z = ends_of(z_low_d, z_high_d, x, 0)
            beside = (d[0], d[2]) + around(
                d[1], coefficient(edge_row(0, x, 0)), coefficient(edge_row(1, x, 0)), low_z, high_z
            )
            faces = [(0.5 * TIME_STEP) * (d[1] + n) for n in beside]
            for f in range(F):
                v = grid[pl.ds(row_of(x, f), 16), :]
                low_z, high_z = ends_of(z_low, z_high, x, f)
                near = (
                    grid[pl.ds(row_of(x - 1, f), 16), :],
                    grid[pl.ds(row_of(x + 1, f), 16), :],
                ) + around(v, edge_row(0, x, f), edge_row(1, x, f), low_z, high_z)
                total = faces[0] * (near[0] - v)
                for a, n in zip(faces[1:], near[1:]):
                    total = total + a * (n - v)
                c = emit(x, f, v, DIFFUSION[f] * total, c)
            return c

        return lax.fori_loop(0, 16, plane, start)

    def ends_of_plane(x, f, v, ends):
        for half in range(2):
            ends = pack_z(x, f, half, v[half * 8 : half * 8 + 8], ends)
        return ends

    zero = jnp.zeros((8, 128), jnp.float32)

    def first_ends(x, ends):
        for f in range(F):
            ends = ends_of_plane(x, f, grid0[pl.ds(row_of(x, f), 16), :], ends)
        return ends

    exchange(0, grid0, lax.fori_loop(0, 16, first_ends, (zero, zero)))

    def keep(x, f, v, change, ends):
        w = v + change
        grid1[pl.ds(row_of(x, f), 16), :] = w
        return ends_of_plane(x, f, w, ends)

    exchange(1, grid1, section(0, grid0, keep, (zero, zero)))

    def finish(x, f, w, change, c):
        out[f, x] = 0.5 * grid0[pl.ds(row_of(x, f), 16), :] + 0.5 * (w + change)
        return c

    section(1, grid1, finish, 0)
    sent = send.at[pl.ds(2, 126)]
    pltpu.make_async_copy(sent, sent, send_sem).wait()


def body(old_fields, new_owner, old_owner):
    boxes = old_fields.reshape(64, 4, 4, 128).transpose(0, 2, 1, 3).reshape(64, 2, 8, 128)
    f32 = jnp.float32
    return pl.pallas_call(
        kernel,
        out_shape=jax.ShapeDtypeStruct((F, 16, 16, 128), f32),
        in_specs=[
            pl.BlockSpec(memory_space=pl.ANY),
            pl.BlockSpec(memory_space=pltpu.SMEM),
            pl.BlockSpec(memory_space=pltpu.SMEM),
        ],
        out_specs=pl.BlockSpec(memory_space=pltpu.VMEM),
        scratch_shapes=[
            pltpu.VMEM((64, 2, 8, 128), f32),
            pltpu.VMEM((128, 2, 8, 128), f32),
            pltpu.VMEM((128, 2, 8, 128), f32),
            pltpu.VMEM((10 * PAIR, 128), f32),
            pltpu.VMEM((10 * PAIR, 128), f32),
            pltpu.VMEM((18 * 16, 128), f32),
            pltpu.VMEM((2, 2, 64, 128), f32),
            pltpu.VMEM((2, 2, 64, 128), f32),
            pltpu.VMEM((2, 2, 8, 128), f32),
            pltpu.VMEM((2, 2, 64, 128), f32),
            pltpu.VMEM((2, 2, 64, 128), f32),
            pltpu.VMEM((2, 2, 8, 128), f32),
            pltpu.VMEM((3, 8, 128), jnp.int32),
            pltpu.SMEM((3, 8, 128), jnp.int32),
            pltpu.SemaphoreType.DMA,
            pltpu.SemaphoreType.DMA((2,)),
            pltpu.SemaphoreType.DMA,
            pltpu.SemaphoreType.DMA,
            pltpu.SemaphoreType.DMA((2, 3, 2)),
            pltpu.SemaphoreType.DMA((2, 3, 2)),
        ],
        compiler_params=pltpu.CompilerParams(
            collective_id=0, has_side_effects=True, vmem_limit_bytes=32 * 2**20
        ),
        name="move_and_diffuse",
    )(boxes, new_owner, old_owner)


def solution(mesh):
    return jax.shard_map(
        body,
        mesh=mesh,
        in_specs=(P(("gx", "gy", "gz"), None, None), P(("gx", "gy", "gz")), P(("gx", "gy", "gz"))),
        out_specs=P(None, "gx", "gy", "gz"),
        check_vma=False,
    )
```

```python
import jax
import jax.numpy as jnp
from jax import lax
from jax.experimental import pallas as pl
from jax.experimental.pallas import tpu as pltpu
from jax.sharding import PartitionSpec as P

DIFFUSION = (1.0, 3.3, 0.9, 1.2)
TIME_STEP = 0.012
MESH = pl.DeviceIdType.MESH
F = 4
CHUNKS = 2
PER = F // CHUNKS
PARTS = (PER + 1) // 2
UNROLL = 2
UNROLL_SETS = 2
SLOT = PER * 8
EDGE = 16
STRIDE = 24
GRID = (EDGE + 2) * STRIDE + 8

OTHERS = sorted(
    [(c, y, z) for c in range(2) for y in range(4) for z in range(8) if c or y or z],
    key=lambda d: -d[0] - min(d[1], 4 - d[1]) - min(d[2], 8 - d[2]),
)


def number(c, y, z):
    return (c * 4 + y % 4) * 8 + z % 8


def coefficient(t):
    return t * jnp.sqrt(t)


def kernel(
    old_hbm, new_hbm, own_hbm, out,
    old, send, recv, grid0, grid1, diff, coef, fy, fz, hy, hz, index_v, index_s, new_owner, old_owner,
    old_sem, owner_sem, index_sem, send_sem, recv_sem, face_send, face_recv,
):
    gx, gy, gz = lax.axis_index("gx"), lax.axis_index("gy"), lax.axis_index("gz")
    core, cy = gx % 2, gx // 2
    grids = (grid0, grid1)

    def peer(c, y, z):
        where = {}
        if c or y:
            where["gx"] = ((cy + y) % 4) * 2 + (core + c) % 2
        if z:
            where["gz"] = (gz + z) % 8
        return where

    barrier = pltpu.get_barrier_semaphore()
    for d in OTHERS:
        pl.semaphore_signal(barrier, inc=1, device_id=peer(*d), device_id_type=MESH)
    for y in (1, 3):
        pl.semaphore_signal(barrier, inc=1, device_id={"gy": (gy + y) % 4}, device_id_type=MESH)
    loads = [
        pltpu.make_async_copy(new_hbm, new_owner, owner_sem.at[0]),
        pltpu.make_async_copy(own_hbm, old_owner, owner_sem.at[1]),
        pltpu.make_async_copy(old_hbm, old.at[pl.ds(16, 1024)], old_sem),
    ]
    for load in loads:
        load.start()
    zeros = jnp.zeros((16, 128), jnp.float32)
    old[pl.ds(0, 16), :] = zeros
    old[pl.ds(1040, 16), :] = zeros
    for k in range(CHUNKS):
        recv[k][pl.ds(0, 8), :] = zeros[:8]
        recv[k][pl.ds(8 + 64 * SLOT, 8), :] = zeros[:8]

    lane = lax.broadcasted_iota(jnp.int32, (8, 128), 1)
    upper = lax.broadcasted_iota(jnp.int32, (8, 128), 0) < 4
    loads[0].wait()

    def leaving(i, c):
        first, last = c
        hit = lane == new_owner[i]
        return jnp.where(hit & (first < 0), i, first), jnp.where(hit, i, last)

    none = jnp.full((8, 128), -1, jnp.int32)
    first, last = lax.fori_loop(0, 64, leaving, (none, none), unroll=8)
    index_v[0] = jnp.maximum(first, 0) * 16
    index_v[1] = jnp.maximum(last, 0) * 16
    to_s = pltpu.make_async_copy(index_v.at[pl.ds(0, 2)], index_s.at[pl.ds(0, 2)], index_sem.at[0])
    to_s.start()
    loads[2].wait()
    to_s.wait()

    def pack(r, c):
        px = ((cy + (r // 8) % 4) % 4) * 2 + (core + r // 32) % 2
        owner = px * 8 + (gz + r) % 8
        a, b = index_s[0, 0, owner], index_s[1, 0, owner]
        for f in range(F):
            va = old[pl.ds(16 + a + f, 8, stride=4), :]
            vb = old[pl.ds(b + f, 8, stride=4), :]
            row = pl.multiple_of(r * SLOT + (f % PER) * 8, 8)
            send[f // PER, pl.ds(row, 8), :] = jnp.where(upper, va, vb)
        return c

    lax.fori_loop(0, 64, pack, 0, unroll=4)
    for k in range(CHUNKS):
        recv[k][pl.ds(8, SLOT), :] = send[k, pl.ds(0, SLOT), :]

    pl.semaphore_wait(barrier, len(OTHERS) + 2)
    for k in range(CHUNKS):
        for c, y, z in OTHERS:
            pltpu.make_async_remote_copy(
                src_ref=send.at[k, pl.ds(number(c, y, z) * SLOT, SLOT)],
                dst_ref=recv[k].at[pl.ds(8 + number(c, -y, -z) * SLOT, SLOT)],
                send_sem=send_sem.at[k],
                recv_sem=recv_sem.at[k],
                device_id=peer(c, y, z),
                device_id_type=MESH,
            ).start()

    loads[1].wait()

    def owners(i, c):
        return jnp.where(lane == i, old_owner[i], c)

    owner = lax.fori_loop(0, 64, owners, none, unroll=8)

    def ranks(i, c):
        return jnp.where((lane > i) & (owner == old_owner[i]), 4, c)

    rank = lax.fori_loop(0, 64, ranks, jnp.zeros((8, 128), jnp.int32), unroll=8)
    ox, oz = owner // 8, owner % 8
    slot = ((ox % 2 - core + 2) % 2 * 4 + (ox // 2 - cy + 4) % 4) * 8 + (oz - gz + 8) % 8
    index_v[2] = slot * SLOT + rank
    to_s = pltpu.make_async_copy(index_v.at[pl.ds(2, 1)], index_s.at[pl.ds(2, 1)], index_sem.at[1])
    to_s.start()
    to_s.wait()

    def arrived(k):
        everyone = recv[k].at[pl.ds(8 + SLOT, 63 * SLOT)]
        pltpu.make_async_copy(everyone, everyone, recv_sem.at[k]).wait()

    bits = [((lane // 8) & step) != 0 for step in (1, 2, 4, 8)]

    def reorder(k):
        def one(s, c):
            f, by = s // 2, s % 2
            v = []
            for bz in range(16):
                a = index_s[2, 0, by * 16 + bz] + f * 8
                b = index_s[2, 0, by * 16 + bz + 32] + f * 8
                box = jnp.where(upper, recv[k][pl.ds(8 + a, 8), :], recv[k][pl.ds(4 + b, 8), :])
                v.append(pltpu.roll(box, 8 * bz, 1) if bz else box)
            for n, bit in enumerate(bits):
                v = [jnp.where(bit, v[(i + (1 << n)) % 16], v[i]) for i in range(16)]
            for g in range(16):
                start = (g // 8 + 1) * STRIDE + 8 + by * 8 + g % 8
                value = pltpu.roll(v[16 - g], 128 - 8 * g, 1) if g else v[0]
                grid0[k * PER + f, pl.ds(start, 8, stride=2 * STRIDE), :] = value
            return c

        lax.fori_loop(0, 2 * PER, one, 0, unroll=UNROLL_SETS)

    def rows(x, y=0):
        if y:
            return pl.ds((x + 1) * STRIDE + 8 + y, EDGE)
        return pl.ds(pl.multiple_of((x + 1) * STRIDE + 8, 8), EDGE)

    def pack_z(x, f, v, ends):
        ends = list(ends)
        for half in range(2):
            twice = (f % 2) * 64 + x * 4 + half * 2
            here = ((lane + 1 - twice) & 127) < 2
            ends[f // 2] = jnp.where(here, pltpu.roll(v[half * 8 : half * 8 + 8], twice, 1), ends[f // 2])
        return tuple(ends)

    def exchange(s, k, ends):
        grid = grids[s]
        fields = pl.ds(k * PER, PER)
        for n, value in enumerate(ends):
            fz[s, k, pl.ds(n * 8, 8)] = value
        copies = []

        def send_face(n, side, axis, here, size, source, target):
            copy = pltpu.make_async_remote_copy(
                src_ref=source,
                dst_ref=target,
                send_sem=face_send.at[s, k, n, side],
                recv_sem=face_recv.at[s, k, n, 1 - side],
                device_id={axis: (here + (1 if side else size - 1)) % size},
                device_id_type=MESH,
            )
            copy.start()
            copies.append(copy)

        for side in range(2):
            send_face(0, side, "gz", gz, 8, fz.at[s, k], hz.at[s, k, 1 - side])
        for side in range(2):
            source = grid.at[fields, pl.ds(STRIDE * (16 if side else 1) + 8, EDGE)]
            target = grid.at[fields, pl.ds(STRIDE * (0 if side else 17) + 8, EDGE)]
            send_face(2, side, "gx", gx, 8, source, target)
        for side in range(2):
            for f in range(PER):
                for part in range(2):
                    fy[s, k, side, pl.ds(f * 16 + part * 8, 8)] = grid[
                        k * PER + f, pl.ds((part * 8 + 1) * STRIDE + 8 + side * 15, 8, stride=STRIDE), :
                    ]
            send_face(1, side, "gy", gy, 4, fy.at[s, k, side], hy.at[s, k, 1 - side])
        everything.extend(copies)
        return copies

    odd = lane % 2 == 1

    def receive(s, k, copies):
        for copy in copies:
            copy.wait_recv()
        for side in range(2):
            for f in range(PER):
                for part in range(2):
                    start = (part * 8 + 1) * STRIDE + (24 if side else 7)
                    grids[s][k * PER + f, pl.ds(start, 8, stride=STRIDE), :] = hy[
                        s, k, side, pl.ds(f * 16 + part * 8, 8)
                    ]
        return [
            jnp.where(odd, hz[s, k, 0, pl.ds(n * 8, 8)], pltpu.roll(hz[s, k, 1, pl.ds(n * 8, 8)], 126, 1))
            for n in range(PARTS)
        ]

    wide = lax.broadcasted_iota(jnp.int32, (16, 128), 1)

    def beside_z(v, edges, x, f):
        twice = (f % 2) * 64 + x * 4
        edge = jnp.concatenate([pltpu.roll(edges[f // 2], (129 - twice - 2 * h) % 128, 1) for h in range(2)], 0)
        return (
            jnp.where(wide == 0, edge, pltpu.roll(v, 1, 1)),
            jnp.where(wide == 127, edge, pltpu.roll(v, 127, 1)),
        )

    def coefficients(s, edges):
        grid = grids[s]

        def diffusivity(x, c):
            part = pl.ds(pl.multiple_of(x * STRIDE, 8), STRIDE)
            diff[part, :] = coefficient(grid[0, part, :])
            return c

        lax.fori_loop(0, 18, diffusivity, 0, unroll=3)
        edges = [coefficient(edge) for edge in edges]

        def plane(x, c):
            d = diff[rows(x), :]
            near = (diff[rows(x - 1), :], diff[rows(x + 1), :], diff[rows(x, -1), :], diff[rows(x, 1), :])
            for n, value in enumerate(near + beside_z(d, edges, x, 0)):
                coef[s, n, pl.ds(pl.multiple_of(x * EDGE, EDGE), EDGE), :] = (0.5 * TIME_STEP) * (d + value)
            return c

        lax.fori_loop(0, 16, plane, 0, unroll=UNROLL)

    def section(s, k, copies, emit, start):
        grid = grids[s]
        edges = receive(s, k, copies)
        if k == 0:
            coefficients(s, edges)

        def plane(x, c):
            faces = [coef[s, n, pl.ds(pl.multiple_of(x * EDGE, EDGE), EDGE), :] for n in range(6)]
            for f in range(PER):
                field = k * PER + f
                v = grid[field, rows(x), :]
                near = (
                    grid[field, rows(x - 1), :],
                    grid[field, rows(x + 1), :],
                    grid[field, rows(x, -1), :],
                    grid[field, rows(x, 1), :],
                ) + beside_z(v, edges, x, f)
                total = faces[0] * (near[0] - v)
                for a, n in zip(faces[1:], near[1:]):
                    total = total + a * (n - v)
                c = emit(x, f, v, DIFFUSION[field] * total, c)
            return c

        return lax.fori_loop(0, 16, plane, start, unroll=UNROLL)

    nothing = (jnp.zeros((8, 128), jnp.float32),) * PARTS
    everything = []

    def to_grid(k):
        arrived(k)
        reorder(k)

        def first_ends(x, ends):
            for f in range(PER):
                ends = pack_z(x, f, grid0[k * PER + f, rows(x), :], ends)
            return ends

        return exchange(0, k, lax.fori_loop(0, 16, first_ends, nothing, unroll=4))

    def first_section(k, copies):
        def keep(x, f, v, change, ends):
            w = v + change
            grid1[k * PER + f, rows(x), :] = w
            return pack_z(x, f, w, ends)

        return exchange(1, k, section(0, k, copies, keep, nothing))

    def second_section(k, copies):
        def finish(x, f, w, change, c):
            out[k * PER + f, x] = 0.5 * grid0[k * PER + f, rows(x), :] + 0.5 * (w + change)
            return c

        section(1, k, copies, finish, 0)

    faces = [to_grid(k) for k in range(CHUNKS)]
    faces = [first_section(k, faces[k]) for k in range(CHUNKS)]
    for k in range(CHUNKS):
        second_section(k, faces[k])
    for copy in everything:
        copy.wait_send()
    for k in range(CHUNKS):
        sent = send.at[k, pl.ds(SLOT, 63 * SLOT)]
        pltpu.make_async_copy(sent, sent, send_sem.at[k]).wait()


def body(old_fields, new_owner, old_owner):
    boxes = old_fields.reshape(64, 4, 4, 128).transpose(0, 2, 1, 3).reshape(1024, 128)
    f32 = jnp.float32
    operands = [pltpu.with_memory_space_constraint(v, pltpu.HBM) for v in (boxes, new_owner, old_owner)]
    return pl.pallas_call(
        kernel,
        out_shape=jax.ShapeDtypeStruct((F, EDGE, EDGE, 128), f32),
        in_specs=[pl.BlockSpec(memory_space=pltpu.HBM)] * 3,
        out_specs=pl.BlockSpec(memory_space=pltpu.VMEM),
        scratch_shapes=[
            pltpu.VMEM((1056, 128), f32),
            pltpu.VMEM((CHUNKS, 64 * SLOT, 128), f32),
            [pltpu.VMEM((64 * SLOT + 16, 128), f32)] * CHUNKS,
            pltpu.VMEM((F, GRID, 128), f32),
            pltpu.VMEM((F, GRID, 128), f32),
            pltpu.VMEM((EDGE * STRIDE + 3 * STRIDE, 128), f32),
            pltpu.VMEM((2, 6, EDGE * EDGE, 128), f32),
            pltpu.VMEM((2, CHUNKS, 2, PER * 16, 128), f32),
            pltpu.VMEM((2, CHUNKS, PARTS * 8, 128), f32),
            pltpu.VMEM((2, CHUNKS, 2, PER * 16, 128), f32),
            pltpu.VMEM((2, CHUNKS, 2, PARTS * 8, 128), f32),
            pltpu.VMEM((3, 8, 128), jnp.int32),
            pltpu.SMEM((3, 8, 128), jnp.int32),
            pltpu.SMEM((64,), jnp.int32),
            pltpu.SMEM((64,), jnp.int32),
            pltpu.SemaphoreType.DMA,
            pltpu.SemaphoreType.DMA((2,)),
            pltpu.SemaphoreType.DMA((2,)),
            pltpu.SemaphoreType.DMA((CHUNKS,)),
            pltpu.SemaphoreType.DMA((CHUNKS,)),
            pltpu.SemaphoreType.DMA((2, CHUNKS, 3, 2)),
            pltpu.SemaphoreType.DMA((2, CHUNKS, 3, 2)),
        ],
        compiler_params=pltpu.CompilerParams(
            collective_id=0, has_side_effects=True, vmem_limit_bytes=32 * 2**20
        ),
        name="move_and_diffuse",
    )(*operands)


def solution(mesh):
    return jax.shard_map(
        body,
        mesh=mesh,
        in_specs=(P(("gx", "gy", "gz"), None, None), P(("gx", "gy", "gz")), P(("gx", "gy", "gz"))),
        out_specs=P(None, "gx", "gy", "gz"),
        check_vma=False,
    )
```

```python
import jax
import jax.numpy as jnp
from jax import lax
from jax.experimental import pallas as pl
from jax.experimental.pallas import tpu as pltpu
from jax.sharding import PartitionSpec as P

DIFFUSION = (1.0, 3.3, 0.9, 1.2)
TIME_STEP = 0.012
MESH = pl.DeviceIdType.MESH
F = 4
FIELDS = ((0, 1, 2), (3,))
CHUNKS = len(FIELDS)
SLOT = [8 * len(fields) for fields in FIELDS]
PARTS = [(len(fields) + 1) // 2 for fields in FIELDS]
UNROLL = 8
EDGE = 16
STRIDE = 24
GRID = (EDGE + 2) * STRIDE + 8

OTHERS = sorted(
    [(c, y, z) for c in range(2) for y in range(4) for z in range(8) if c or y or z],
    key=lambda d: -d[0] - min(d[1], 4 - d[1]) - min(d[2], 8 - d[2]),
)


def number(c, y, z):
    return (c * 4 + y % 4) * 8 + z % 8


def coefficient(t):
    return t * jnp.sqrt(t)


def kernel(
    old_hbm, new_hbm, own_hbm, out,
    old, send, recv, grid0, grid1, diff, coef, fy, fz, hy, hz, index_v, index_s, new_owner, old_owner,
    old_sem, owner_sem, index_sem, send_sem, recv_sem, face_send, face_recv,
):
    gx, gy, gz = lax.axis_index("gx"), lax.axis_index("gy"), lax.axis_index("gz")
    core, cy = gx % 2, gx // 2
    grids = (grid0, grid1)

    def peer(c, y, z):
        where = {}
        if c or y:
            where["gx"] = ((cy + y) % 4) * 2 + (core + c) % 2
        if z:
            where["gz"] = (gz + z) % 8
        return where

    barrier = pltpu.get_barrier_semaphore()
    for d in OTHERS:
        pl.semaphore_signal(barrier, inc=1, device_id=peer(*d), device_id_type=MESH)
    for y in (1, 3):
        pl.semaphore_signal(barrier, inc=1, device_id={"gy": (gy + y) % 4}, device_id_type=MESH)
    loads = [
        pltpu.make_async_copy(new_hbm, new_owner, owner_sem.at[0]),
        pltpu.make_async_copy(own_hbm, old_owner, owner_sem.at[1]),
        pltpu.make_async_copy(old_hbm, old.at[pl.ds(16, 1024)], old_sem),
    ]
    for load in loads:
        load.start()
    zeros = jnp.zeros((16, 128), jnp.float32)
    old[pl.ds(0, 16), :] = zeros
    old[pl.ds(1040, 16), :] = zeros
    for k in range(CHUNKS):
        recv[k][pl.ds(0, 8), :] = zeros[:8]
        recv[k][pl.ds(8 + 64 * SLOT[k], 8), :] = zeros[:8]

    lane = lax.broadcasted_iota(jnp.int32, (8, 128), 1)
    upper = lax.broadcasted_iota(jnp.int32, (8, 128), 0) < 4
    loads[0].wait()

    def leaving(i, c):
        first, last = c
        hit = lane == new_owner[i]
        return jnp.where(hit & (first < 0), i, first), jnp.where(hit, i, last)

    none = jnp.full((8, 128), -1, jnp.int32)
    first, last = lax.fori_loop(0, 64, leaving, (none, none), unroll=8)
    index_v[0] = jnp.maximum(first, 0) * 16
    index_v[1] = jnp.maximum(last, 0) * 16
    to_s = pltpu.make_async_copy(index_v.at[pl.ds(0, 2)], index_s.at[pl.ds(0, 2)], index_sem.at[0])
    to_s.start()
    loads[2].wait()
    to_s.wait()

    def pack(r, c):
        px = ((cy + (r // 8) % 4) % 4) * 2 + (core + r // 32) % 2
        owner = px * 8 + (gz + r) % 8
        a, b = index_s[0, 0, owner], index_s[1, 0, owner]
        for f in range(F):
            va = old[pl.ds(16 + a + f, 8, stride=4), :]
            vb = old[pl.ds(b + f, 8, stride=4), :]
            k = next(k for k in range(CHUNKS) if f in FIELDS[k])
            row = pl.multiple_of(r * SLOT[k] + FIELDS[k].index(f) * 8, 8)
            send[k][pl.ds(row, 8), :] = jnp.where(upper, va, vb)
        return c

    lax.fori_loop(0, 64, pack, 0, unroll=4)
    for k in range(CHUNKS):
        recv[k][pl.ds(8, SLOT[k]), :] = send[k][pl.ds(0, SLOT[k]), :]

    pl.semaphore_wait(barrier, len(OTHERS) + 2)
    for k in range(CHUNKS):
        for c, y, z in OTHERS:
            pltpu.make_async_remote_copy(
                src_ref=send[k].at[pl.ds(number(c, y, z) * SLOT[k], SLOT[k])],
                dst_ref=recv[k].at[pl.ds(8 + number(c, -y, -z) * SLOT[k], SLOT[k])],
                send_sem=send_sem.at[k],
                recv_sem=recv_sem.at[k],
                device_id=peer(c, y, z),
                device_id_type=MESH,
            ).start()

    loads[1].wait()

    def owners(i, c):
        return jnp.where(lane == i, old_owner[i], c)

    owner = lax.fori_loop(0, 64, owners, none, unroll=8)

    def ranks(i, c):
        return jnp.where((lane > i) & (owner == old_owner[i]), 4, c)

    rank = lax.fori_loop(0, 64, ranks, jnp.zeros((8, 128), jnp.int32), unroll=8)
    ox, oz = owner // 8, owner % 8
    slot = ((ox % 2 - core + 2) % 2 * 4 + (ox // 2 - cy + 4) % 4) * 8 + (oz - gz + 8) % 8
    for k in range(CHUNKS):
        index_v[2 + k] = slot * SLOT[k] + rank
    to_s = pltpu.make_async_copy(
        index_v.at[pl.ds(2, CHUNKS)], index_s.at[pl.ds(2, CHUNKS)], index_sem.at[1]
    )
    to_s.start()
    to_s.wait()

    def arrived(k):
        everyone = recv[k].at[pl.ds(8 + SLOT[k], 63 * SLOT[k])]
        pltpu.make_async_copy(everyone, everyone, recv_sem.at[k]).wait()

    bits = [((lane // 8) & step) != 0 for step in (1, 2, 4, 8)]

    def reorder(k):
        def one(s, c):
            f, by = s // 2, s % 2
            v = []
            for bz in range(16):
                a = index_s[2 + k, 0, by * 16 + bz] + f * 8
                b = index_s[2 + k, 0, by * 16 + bz + 32] + f * 8
                box = jnp.where(upper, recv[k][pl.ds(8 + a, 8), :], recv[k][pl.ds(4 + b, 8), :])
                v.append(pltpu.roll(box, 8 * bz, 1) if bz else box)
            for n, bit in enumerate(bits):
                v = [jnp.where(bit, v[(i + (1 << n)) % 16], v[i]) for i in range(16)]
            for g in range(16):
                start = (g // 8 + 1) * STRIDE + 8 + by * 8 + g % 8
                value = pltpu.roll(v[16 - g], 128 - 8 * g, 1) if g else v[0]
                grid0[FIELDS[k][0] + f, pl.ds(start, 8, stride=2 * STRIDE), :] = value
            return c

        lax.fori_loop(0, 2 * len(FIELDS[k]), one, 0, unroll=2)

    def rows(x, y=0):
        if y:
            return pl.ds((x + 1) * STRIDE + 8 + y, EDGE)
        return pl.ds(pl.multiple_of((x + 1) * STRIDE + 8, 8), EDGE)

    def pack_z(x, f, v, ends):
        ends = list(ends)
        for half in range(2):
            twice = (f % 2) * 64 + x * 4 + half * 2
            here = ((lane + 1 - twice) & 127) < 2
            ends[f // 2] = jnp.where(here, pltpu.roll(v[half * 8 : half * 8 + 8], twice, 1), ends[f // 2])
        return tuple(ends)

    def exchange(s, k, ends):
        grid = grids[s]
        fields = pl.ds(FIELDS[k][0], len(FIELDS[k]))
        for n, value in enumerate(ends):
            fz[k][s, pl.ds(n * 8, 8)] = value
        copies = []

        def send_face(n, side, axis, here, size, source, target):
            copy = pltpu.make_async_remote_copy(
                src_ref=source,
                dst_ref=target,
                send_sem=face_send.at[s, k, n, side],
                recv_sem=face_recv.at[s, k, n, 1 - side],
                device_id={axis: (here + (1 if side else size - 1)) % size},
                device_id_type=MESH,
            )
            copy.start()
            copies.append(copy)

        for side in range(2):
            send_face(0, side, "gz", gz, 8, fz[k].at[s], hz[k].at[s, 1 - side])
        for side in range(2):
            source = grid.at[fields, pl.ds(STRIDE * (16 if side else 1) + 8, EDGE)]
            target = grid.at[fields, pl.ds(STRIDE * (0 if side else 17) + 8, EDGE)]
            send_face(2, side, "gx", gx, 8, source, target)
        for side in range(2):
            for f, field in enumerate(FIELDS[k]):
                for part in range(2):
                    fy[k][s, side, pl.ds(f * 16 + part * 8, 8)] = grid[
                        field, pl.ds((part * 8 + 1) * STRIDE + 8 + side * 15, 8, stride=STRIDE), :
                    ]
            send_face(1, side, "gy", gy, 4, fy[k].at[s, side], hy[k].at[s, 1 - side])
        everything.extend(copies)
        return copies

    odd = lane % 2 == 1

    def receive(s, k, copies):
        for copy in copies:
            copy.wait_recv()
        for side in range(2):
            for f, field in enumerate(FIELDS[k]):
                for part in range(2):
                    start = (part * 8 + 1) * STRIDE + (24 if side else 7)
                    grids[s][field, pl.ds(start, 8, stride=STRIDE), :] = hy[k][
                        s, side, pl.ds(f * 16 + part * 8, 8)
                    ]
        return [
            jnp.where(odd, hz[k][s, 0, pl.ds(n * 8, 8)], pltpu.roll(hz[k][s, 1, pl.ds(n * 8, 8)], 126, 1))
            for n in range(PARTS[k])
        ]

    wide = lax.broadcasted_iota(jnp.int32, (16, 128), 1)

    def beside_z(v, edges, x, f):
        twice = (f % 2) * 64 + x * 4
        edge = jnp.concatenate([pltpu.roll(edges[f // 2], (129 - twice - 2 * h) % 128, 1) for h in range(2)], 0)
        return (
            jnp.where(wide == 0, edge, pltpu.roll(v, 1, 1)),
            jnp.where(wide == 127, edge, pltpu.roll(v, 127, 1)),
        )

    def coefficients(s, edges):
        grid = grids[s]

        def diffusivity(x, c):
            part = pl.ds(pl.multiple_of(x * STRIDE, 8), STRIDE)
            diff[part, :] = coefficient(grid[0, part, :])
            return c

        lax.fori_loop(0, 18, diffusivity, 0, unroll=3)
        edges = [coefficient(edge) for edge in edges]

        def plane(x, c):
            d = diff[rows(x), :]
            near = (diff[rows(x - 1), :], diff[rows(x + 1), :], diff[rows(x, -1), :], diff[rows(x, 1), :])
            for n, value in enumerate(near + beside_z(d, edges, x, 0)):
                coef[s, n, pl.ds(pl.multiple_of(x * EDGE, EDGE), EDGE), :] = (0.5 * TIME_STEP) * (d + value)
            return c

        lax.fori_loop(0, 16, plane, 0, unroll=UNROLL)

    def section(s, k, copies, emit, start):
        grid = grids[s]
        edges = receive(s, k, copies)
        if k == 0:
            coefficients(s, edges)

        def plane(x, c):
            faces = [coef[s, n, pl.ds(pl.multiple_of(x * EDGE, EDGE), EDGE), :] for n in range(6)]
            for f, field in enumerate(FIELDS[k]):
                v = grid[field, rows(x), :]
                near = (
                    grid[field, rows(x - 1), :],
                    grid[field, rows(x + 1), :],
                    grid[field, rows(x, -1), :],
                    grid[field, rows(x, 1), :],
                ) + beside_z(v, edges, x, f)
                total = faces[0] * (near[0] - v)
                for a, n in zip(faces[1:], near[1:]):
                    total = total + a * (n - v)
                c = emit(x, f, field, v, DIFFUSION[field] * total, c)
            return c

        return lax.fori_loop(0, 16, plane, start, unroll=UNROLL)

    nothing = [(jnp.zeros((8, 128), jnp.float32),) * PARTS[k] for k in range(CHUNKS)]
    everything = []

    def to_grid(k):
        arrived(k)
        reorder(k)

        def first_ends(x, ends):
            for f, field in enumerate(FIELDS[k]):
                ends = pack_z(x, f, grid0[field, rows(x), :], ends)
            return ends

        return exchange(0, k, lax.fori_loop(0, 16, first_ends, nothing[k], unroll=4))

    def first_section(k, copies):
        def keep(x, f, field, v, change, ends):
            w = v + change
            grid1[field, rows(x), :] = w
            return pack_z(x, f, w, ends)

        return exchange(1, k, section(0, k, copies, keep, nothing[k]))

    def second_section(k, copies):
        def finish(x, f, field, w, change, c):
            out[field, x] = 0.5 * grid0[field, rows(x), :] + 0.5 * (w + change)
            return c

        section(1, k, copies, finish, 0)

    faces = [to_grid(k) for k in range(CHUNKS)]
    faces = [first_section(k, faces[k]) for k in range(CHUNKS)]
    for k in range(CHUNKS):
        second_section(k, faces[k])
    for copy in everything:
        copy.wait_send()
    for k in range(CHUNKS):
        sent = send[k].at[pl.ds(SLOT[k], 63 * SLOT[k])]
        pltpu.make_async_copy(sent, sent, send_sem.at[k]).wait()


def body(old_fields, new_owner, old_owner):
    boxes = old_fields.reshape(64, 4, 4, 128).transpose(0, 2, 1, 3).reshape(1024, 128)
    f32 = jnp.float32
    operands = [pltpu.with_memory_space_constraint(v, pltpu.HBM) for v in (boxes, new_owner, old_owner)]
    return pl.pallas_call(
        kernel,
        out_shape=jax.ShapeDtypeStruct((F, EDGE, EDGE, 128), f32),
        in_specs=[pl.BlockSpec(memory_space=pltpu.HBM)] * 3,
        out_specs=pl.BlockSpec(memory_space=pltpu.VMEM),
        scratch_shapes=[
            pltpu.VMEM((1056, 128), f32),
            [pltpu.VMEM((64 * rows, 128), f32) for rows in SLOT],
            [pltpu.VMEM((64 * rows + 16, 128), f32) for rows in SLOT],
            pltpu.VMEM((F, GRID, 128), f32),
            pltpu.VMEM((F, GRID, 128), f32),
            pltpu.VMEM((EDGE * STRIDE + 3 * STRIDE, 128), f32),
            pltpu.VMEM((2, 6, EDGE * EDGE, 128), f32),
            [pltpu.VMEM((2, 2, rows * 2, 128), f32) for rows in SLOT],
            [pltpu.VMEM((2, parts * 8, 128), f32) for parts in PARTS],
            [pltpu.VMEM((2, 2, rows * 2, 128), f32) for rows in SLOT],
            [pltpu.VMEM((2, 2, parts * 8, 128), f32) for parts in PARTS],
            pltpu.VMEM((2 + CHUNKS, 8, 128), jnp.int32),
            pltpu.SMEM((2 + CHUNKS, 8, 128), jnp.int32),
            pltpu.SMEM((64,), jnp.int32),
            pltpu.SMEM((64,), jnp.int32),
            pltpu.SemaphoreType.DMA,
            pltpu.SemaphoreType.DMA((2,)),
            pltpu.SemaphoreType.DMA((2,)),
            pltpu.SemaphoreType.DMA((CHUNKS,)),
            pltpu.SemaphoreType.DMA((CHUNKS,)),
            pltpu.SemaphoreType.DMA((2, CHUNKS, 3, 2)),
            pltpu.SemaphoreType.DMA((2, CHUNKS, 3, 2)),
        ],
        compiler_params=pltpu.CompilerParams(
            collective_id=0, has_side_effects=True, vmem_limit_bytes=32 * 2**20
        ),
        name="move_and_diffuse",
    )(*operands)


def solution(mesh):
    return jax.shard_map(
        body,
        mesh=mesh,
        in_specs=(P(("gx", "gy", "gz"), None, None), P(("gx", "gy", "gz")), P(("gx", "gy", "gz"))),
        out_specs=P(None, "gx", "gy", "gz"),
        check_vma=False,
    )
```

```python
import jax
import jax.numpy as jnp
from jax import lax
from jax.experimental import pallas as pl
from jax.experimental.pallas import tpu as pltpu
from jax.sharding import PartitionSpec as P

DIFFUSION = (1.0, 3.3, 0.9, 1.2)
TIME_STEP = 0.012
MESH = pl.DeviceIdType.MESH
F = 4
FIELDS = ((0, 1, 2), (3,))
CHUNKS = len(FIELDS)
SLOT = [8 * len(fields) for fields in FIELDS]
PARTS = [(len(fields) + 1) // 2 for fields in FIELDS]
UNROLL = 8
EDGE = 16
STRIDE = 24
GRID = (EDGE + 2) * STRIDE + 8

OTHERS = sorted(
    [(c, y, z) for c in range(2) for y in range(4) for z in range(8) if c or y or z],
    key=lambda d: -d[0] - min(d[1], 4 - d[1]) - min(d[2], 8 - d[2]),
)


def hops(c, y, z):
    return c + min(y, 4 - y) + min(z, 8 - z)


def ball(n):
    return [d for d in OTHERS if hops(*d) <= n]


GREET = (2, 2, 3)
KNOWN = (2, 4, 7)


def number(c, y, z):
    return (c * 4 + y % 4) * 8 + z % 8


def coefficient(t):
    return t * jnp.sqrt(t)


def kernel(
    old_hbm, new_hbm, own_hbm, out,
    old, send, recv, grid0, grid1, diff, coef, fy, fz, hy, hz, index_v, index_s, new_owner, old_owner,
    old_sem, owner_sem, index_sem, ready, send_sem, recv_sem, face_send, face_recv,
):
    gx, gy, gz = lax.axis_index("gx"), lax.axis_index("gy"), lax.axis_index("gz")
    core, cy = gx % 2, gx // 2
    grids = (grid0, grid1)

    def peer(c, y, z):
        where = {}
        if c or y:
            where["gx"] = ((cy + y) % 4) * 2 + (core + c) % 2
        if z:
            where["gz"] = (gz + z) % 8
        return where

    barrier = pltpu.get_barrier_semaphore()
    def greet(sem, r):
        for d in ball(GREET[r]):
            pl.semaphore_signal(sem, inc=1, device_id=peer(*d), device_id_type=MESH)

    greet(barrier, 0)
    for y in (1, 3):
        pl.semaphore_signal(barrier, inc=1, device_id={"gy": (gy + y) % 4}, device_id_type=MESH)
    loads = [
        pltpu.make_async_copy(new_hbm, new_owner, owner_sem.at[0]),
        pltpu.make_async_copy(own_hbm, old_owner, owner_sem.at[1]),
        pltpu.make_async_copy(old_hbm, old.at[pl.ds(16, 1024)], old_sem),
    ]
    for load in loads:
        load.start()
    zeros = jnp.zeros((16, 128), jnp.float32)
    old[pl.ds(0, 16), :] = zeros
    old[pl.ds(1040, 16), :] = zeros
    for k in range(CHUNKS):
        recv[k][pl.ds(0, 8), :] = zeros[:8]
        recv[k][pl.ds(8 + 64 * SLOT[k], 8), :] = zeros[:8]

    lane = lax.broadcasted_iota(jnp.int32, (8, 128), 1)
    upper = lax.broadcasted_iota(jnp.int32, (8, 128), 0) < 4
    loads[0].wait()

    def leaving(i, c):
        first, last = c
        hit = lane == new_owner[i]
        return jnp.where(hit & (first < 0), i, first), jnp.where(hit, i, last)

    none = jnp.full((8, 128), -1, jnp.int32)
    first, last = lax.fori_loop(0, 64, leaving, (none, none), unroll=8)
    index_v[0] = jnp.maximum(first, 0) * 16
    index_v[1] = jnp.maximum(last, 0) * 16
    to_s = pltpu.make_async_copy(index_v.at[pl.ds(0, 2)], index_s.at[pl.ds(0, 2)], index_sem.at[0])
    to_s.start()
    loads[2].wait()
    to_s.wait()

    def pack(r, c):
        px = ((cy + (r // 8) % 4) % 4) * 2 + (core + r // 32) % 2
        owner = px * 8 + (gz + r) % 8
        a, b = index_s[0, 0, owner], index_s[1, 0, owner]
        for f in range(F):
            va = old[pl.ds(16 + a + f, 8, stride=4), :]
            vb = old[pl.ds(b + f, 8, stride=4), :]
            k = next(k for k in range(CHUNKS) if f in FIELDS[k])
            row = pl.multiple_of(r * SLOT[k] + FIELDS[k].index(f) * 8, 8)
            send[k][pl.ds(row, 8), :] = jnp.where(upper, va, vb)
        return c

    lax.fori_loop(0, 64, pack, 0, unroll=4)
    for k in range(CHUNKS):
        recv[k][pl.ds(8, SLOT[k]), :] = send[k][pl.ds(0, SLOT[k]), :]

    def post(k, near, far):
        for c, y, z in OTHERS:
            if not near < hops(c, y, z) <= far:
                continue
            pltpu.make_async_remote_copy(
                src_ref=send[k].at[pl.ds(number(c, y, z) * SLOT[k], SLOT[k])],
                dst_ref=recv[k].at[pl.ds(8 + number(c, -y, -z) * SLOT[k], SLOT[k])],
                send_sem=send_sem.at[k],
                recv_sem=recv_sem.at[k],
                device_id=peer(c, y, z),
                device_id_type=MESH,
            ).start()

    last = len(KNOWN) - 1
    for r, far in enumerate(KNOWN):
        if r:
            pl.semaphore_wait(ready.at[r - 1], len(ball(GREET[r])))
        else:
            pl.semaphore_wait(barrier, len(ball(GREET[0])) + 2)
        if r < last:
            greet(ready.at[r], r + 1)
        post(0, KNOWN[r - 1] if r else 0, far)
        if r == 0:
            post(1, 0, 2)
    post(1, 2, 7)

    loads[1].wait()

    def owners(i, c):
        return jnp.where(lane == i, old_owner[i], c)

    owner = lax.fori_loop(0, 64, owners, none, unroll=8)

    def ranks(i, c):
        return jnp.where((lane > i) & (owner == old_owner[i]), 4, c)

    rank = lax.fori_loop(0, 64, ranks, jnp.zeros((8, 128), jnp.int32), unroll=8)
    ox, oz = owner // 8, owner % 8
    slot = ((ox % 2 - core + 2) % 2 * 4 + (ox // 2 - cy + 4) % 4) * 8 + (oz - gz + 8) % 8
    for k in range(CHUNKS):
        index_v[2 + k] = slot * SLOT[k] + rank
    to_s = pltpu.make_async_copy(
        index_v.at[pl.ds(2, CHUNKS)], index_s.at[pl.ds(2, CHUNKS)], index_sem.at[1]
    )
    to_s.start()
    to_s.wait()

    def arrived(k):
        everyone = recv[k].at[pl.ds(8 + SLOT[k], 63 * SLOT[k])]
        pltpu.make_async_copy(everyone, everyone, recv_sem.at[k]).wait()

    bits = [((lane // 8) & step) != 0 for step in (1, 2, 4, 8)]

    def reorder(k):
        def one(s, c):
            f, by = s // 2, s % 2
            v = []
            for bz in range(16):
                a = index_s[2 + k, 0, by * 16 + bz] + f * 8
                b = index_s[2 + k, 0, by * 16 + bz + 32] + f * 8
                box = jnp.where(upper, recv[k][pl.ds(8 + a, 8), :], recv[k][pl.ds(4 + b, 8), :])
                v.append(pltpu.roll(box, 8 * bz, 1) if bz else box)
            for n, bit in enumerate(bits):
                v = [jnp.where(bit, v[(i + (1 << n)) % 16], v[i]) for i in range(16)]
            for g in range(16):
                start = (g // 8 + 1) * STRIDE + 8 + by * 8 + g % 8
                value = pltpu.roll(v[16 - g], 128 - 8 * g, 1) if g else v[0]
                grid0[FIELDS[k][0] + f, pl.ds(start, 8, stride=2 * STRIDE), :] = value
            return c

        lax.fori_loop(0, 2 * len(FIELDS[k]), one, 0, unroll=2)

    def rows(x, y=0):
        if y:
            return pl.ds((x + 1) * STRIDE + 8 + y, EDGE)
        return pl.ds(pl.multiple_of((x + 1) * STRIDE + 8, 8), EDGE)

    def pack_z(x, f, v, ends):
        ends = list(ends)
        for half in range(2):
            twice = (f % 2) * 64 + x * 4 + half * 2
            here = ((lane + 1 - twice) & 127) < 2
            ends[f // 2] = jnp.where(here, pltpu.roll(v[half * 8 : half * 8 + 8], twice, 1), ends[f // 2])
        return tuple(ends)

    def exchange(s, k, ends):
        grid = grids[s]
        fields = pl.ds(FIELDS[k][0], len(FIELDS[k]))
        copies = []

        def send_face(n, side, axis, here, size, source, target):
            copy = pltpu.make_async_remote_copy(
                src_ref=source,
                dst_ref=target,
                send_sem=face_send.at[s, k, n, side],
                recv_sem=face_recv.at[s, k, n, 1 - side],
                device_id={axis: (here + (1 if side else size - 1)) % size},
                device_id_type=MESH,
            )
            copy.start()
            copies.append(copy)

        for side in range(2):
            source = grid.at[fields, pl.ds(STRIDE * (16 if side else 1) + 8, EDGE)]
            target = grid.at[fields, pl.ds(STRIDE * (0 if side else 17) + 8, EDGE)]
            send_face(2, side, "gx", gx, 8, source, target)
        for side in range(2):
            for f, field in enumerate(FIELDS[k]):
                for part in range(2):
                    fy[k][s, side, pl.ds(f * 16 + part * 8, 8)] = grid[
                        field, pl.ds((part * 8 + 1) * STRIDE + 8 + side * 15, 8, stride=STRIDE), :
                    ]
            send_face(1, side, "gy", gy, 4, fy[k].at[s, side], hy[k].at[s, 1 - side])
        if callable(ends):
            ends = ends()
        for n, value in enumerate(ends):
            fz[k][s, pl.ds(n * 8, 8)] = value
        for side in range(2):
            send_face(0, side, "gz", gz, 8, fz[k].at[s], hz[k].at[s, 1 - side])
        everything.extend(copies)
        return copies

    odd = lane % 2 == 1

    def receive(s, k, copies):
        for copy in copies:
            copy.wait_recv()
        for side in range(2):
            for f, field in enumerate(FIELDS[k]):
                for part in range(2):
                    start = (part * 8 + 1) * STRIDE + (24 if side else 7)
                    grids[s][field, pl.ds(start, 8, stride=STRIDE), :] = hy[k][
                        s, side, pl.ds(f * 16 + part * 8, 8)
                    ]
        return [
            jnp.where(odd, hz[k][s, 0, pl.ds(n * 8, 8)], pltpu.roll(hz[k][s, 1, pl.ds(n * 8, 8)], 126, 1))
            for n in range(PARTS[k])
        ]

    wide = lax.broadcasted_iota(jnp.int32, (16, 128), 1)

    def beside_z(v, edges, x, f):
        twice = (f % 2) * 64 + x * 4
        edge = jnp.concatenate([pltpu.roll(edges[f // 2], (129 - twice - 2 * h) % 128, 1) for h in range(2)], 0)
        return (
            jnp.where(wide == 0, edge, pltpu.roll(v, 1, 1)),
            jnp.where(wide == 127, edge, pltpu.roll(v, 127, 1)),
        )

    def coefficients(s, edges):
        grid = grids[s]

        def diffusivity(x, c):
            part = pl.ds(pl.multiple_of(x * STRIDE, 8), STRIDE)
            diff[part, :] = coefficient(grid[0, part, :])
            return c

        lax.fori_loop(0, 18, diffusivity, 0, unroll=3)
        edges = [coefficient(edge) for edge in edges]

        def plane(x, c):
            d = diff[rows(x), :]
            near = (diff[rows(x - 1), :], diff[rows(x + 1), :], diff[rows(x, -1), :], diff[rows(x, 1), :])
            for n, value in enumerate(near + beside_z(d, edges, x, 0)):
                coef[s, n, pl.ds(pl.multiple_of(x * EDGE, EDGE), EDGE), :] = (0.5 * TIME_STEP) * (d + value)
            return c

        lax.fori_loop(0, 16, plane, 0, unroll=UNROLL)

    def section(s, k, copies, emit, start):
        grid = grids[s]
        edges = receive(s, k, copies)
        if k == 0:
            coefficients(s, edges)

        def plane(x, c):
            faces = [coef[s, n, pl.ds(pl.multiple_of(x * EDGE, EDGE), EDGE), :] for n in range(6)]
            for f, field in enumerate(FIELDS[k]):
                v = grid[field, rows(x), :]
                near = (
                    grid[field, rows(x - 1), :],
                    grid[field, rows(x + 1), :],
                    grid[field, rows(x, -1), :],
                    grid[field, rows(x, 1), :],
                ) + beside_z(v, edges, x, f)
                total = faces[0] * (near[0] - v)
                for a, n in zip(faces[1:], near[1:]):
                    total = total + a * (n - v)
                c = emit(x, f, field, v, DIFFUSION[field] * total, c)
            return c

        return lax.fori_loop(0, 16, plane, start, unroll=UNROLL)

    nothing = [(jnp.zeros((8, 128), jnp.float32),) * PARTS[k] for k in range(CHUNKS)]
    everything = []

    def to_grid(k):
        arrived(k)
        reorder(k)

        def first_ends(x, ends):
            for f, field in enumerate(FIELDS[k]):
                ends = pack_z(x, f, grid0[field, rows(x), :], ends)
            return ends

        return exchange(0, k, lambda: lax.fori_loop(0, 16, first_ends, nothing[k], unroll=4))

    def first_section(k, copies):
        def keep(x, f, field, v, change, ends):
            w = v + change
            grid1[field, rows(x), :] = w
            return pack_z(x, f, w, ends)

        return exchange(1, k, section(0, k, copies, keep, nothing[k]))

    def second_section(k, copies):
        def finish(x, f, field, w, change, c):
            out[field, x] = 0.5 * grid0[field, rows(x), :] + 0.5 * (w + change)
            return c

        section(1, k, copies, finish, 0)

    faces = [to_grid(k) for k in range(CHUNKS)]
    faces = [first_section(k, faces[k]) for k in range(CHUNKS)]
    for k in range(CHUNKS):
        second_section(k, faces[k])
    for copy in everything:
        copy.wait_send()
    for k in range(CHUNKS):
        sent = send[k].at[pl.ds(SLOT[k], 63 * SLOT[k])]
        pltpu.make_async_copy(sent, sent, send_sem.at[k]).wait()


def body(old_fields, new_owner, old_owner):
    boxes = old_fields.reshape(64, 4, 4, 128).transpose(0, 2, 1, 3).reshape(1024, 128)
    f32 = jnp.float32
    operands = [pltpu.with_memory_space_constraint(v, pltpu.HBM) for v in (boxes, new_owner, old_owner)]
    return pl.pallas_call(
        kernel,
        out_shape=jax.ShapeDtypeStruct((F, EDGE, EDGE, 128), f32),
        in_specs=[pl.BlockSpec(memory_space=pltpu.HBM)] * 3,
        out_specs=pl.BlockSpec(memory_space=pltpu.VMEM),
        scratch_shapes=[
            pltpu.VMEM((1056, 128), f32),
            [pltpu.VMEM((64 * rows, 128), f32) for rows in SLOT],
            [pltpu.VMEM((64 * rows + 16, 128), f32) for rows in SLOT],
            pltpu.VMEM((F, GRID, 128), f32),
            pltpu.VMEM((F, GRID, 128), f32),
            pltpu.VMEM((EDGE * STRIDE + 3 * STRIDE, 128), f32),
            pltpu.VMEM((2, 6, EDGE * EDGE, 128), f32),
            [pltpu.VMEM((2, 2, rows * 2, 128), f32) for rows in SLOT],
            [pltpu.VMEM((2, parts * 8, 128), f32) for parts in PARTS],
            [pltpu.VMEM((2, 2, rows * 2, 128), f32) for rows in SLOT],
            [pltpu.VMEM((2, 2, parts * 8, 128), f32) for parts in PARTS],
            pltpu.VMEM((2 + CHUNKS, 8, 128), jnp.int32),
            pltpu.SMEM((2 + CHUNKS, 8, 128), jnp.int32),
            pltpu.SMEM((64,), jnp.int32),
            pltpu.SMEM((64,), jnp.int32),
            pltpu.SemaphoreType.DMA,
            pltpu.SemaphoreType.DMA((2,)),
            pltpu.SemaphoreType.DMA((2,)),
            pltpu.SemaphoreType.REGULAR((len(KNOWN),)),
            pltpu.SemaphoreType.DMA((CHUNKS,)),
            pltpu.SemaphoreType.DMA((CHUNKS,)),
            pltpu.SemaphoreType.DMA((2, CHUNKS, 3, 2)),
            pltpu.SemaphoreType.DMA((2, CHUNKS, 3, 2)),
        ],
        compiler_params=pltpu.CompilerParams(
            collective_id=0, has_side_effects=True, vmem_limit_bytes=32 * 2**20
        ),
        name="move_and_diffuse",
    )(*operands)


def solution(mesh):
    return jax.shard_map(
        body,
        mesh=mesh,
        in_specs=(P(("gx", "gy", "gz"), None, None), P(("gx", "gy", "gz")), P(("gx", "gy", "gz"))),
        out_specs=P(None, "gx", "gy", "gz"),
        check_vma=False,
    )
```

```python
import jax
import jax.numpy as jnp
from jax import lax
from jax.experimental import pallas as pl
from jax.experimental.pallas import tpu as pltpu
from jax.sharding import PartitionSpec as P

DIFFUSION = (1.0, 3.3, 0.9, 1.2)
TIME_STEP = 0.012
MESH = pl.DeviceIdType.MESH
F = 4
FIELDS = ((0, 1, 2), (3,))
CHUNKS = len(FIELDS)
SLOT = [8 * len(fields) for fields in FIELDS]
PARTS = [(len(fields) + 1) // 2 for fields in FIELDS]
UNROLL = 8
EDGE = 16
STRIDE = 24
GRID = (EDGE + 2) * STRIDE + 8

OTHERS = sorted(
    [(c, y, z) for c in range(2) for y in range(4) for z in range(8) if c or y or z],
    key=lambda d: -d[0] - min(d[1], 4 - d[1]) - min(d[2], 8 - d[2]),
)


def hops(c, y, z):
    return c + min(y, 4 - y) + min(z, 8 - z)


def ball(n):
    return [d for d in OTHERS if hops(*d) <= n]


GREET = (2, 2, 3)
KNOWN = (2, 4, 7)


def number(c, y, z):
    return (c * 4 + y % 4) * 8 + z % 8


def coefficient(t):
    return t * jnp.sqrt(t)


def kernel(
    old_hbm, new_hbm, own_hbm, out,
    old, send, recv, grid0, grid1, diff, coef, fy, fz, hy, hz, index_v, index_s, new_owner, old_owner,
    old_sem, owner_sem, index_sem, ready, send_sem, recv_sem, face_send, face_recv,
):
    gx, gy, gz = lax.axis_index("gx"), lax.axis_index("gy"), lax.axis_index("gz")
    core, cy = gx % 2, gx // 2
    grids = (grid0, grid1)

    def peer(c, y, z):
        where = {}
        if c or y:
            where["gx"] = ((cy + y) % 4) * 2 + (core + c) % 2
        if z:
            where["gz"] = (gz + z) % 8
        return where

    barrier = pltpu.get_barrier_semaphore()
    def greet(sem, r):
        for d in ball(GREET[r]):
            pl.semaphore_signal(sem, inc=1, device_id=peer(*d), device_id_type=MESH)

    greet(barrier, 0)
    for y in (1, 3):
        pl.semaphore_signal(barrier, inc=1, device_id={"gy": (gy + y) % 4}, device_id_type=MESH)
    loads = [
        pltpu.make_async_copy(new_hbm, new_owner, owner_sem.at[0]),
        pltpu.make_async_copy(own_hbm, old_owner, owner_sem.at[1]),
        pltpu.make_async_copy(old_hbm, old.at[pl.ds(16, 1024)], old_sem),
    ]
    for load in loads:
        load.start()
    zeros = jnp.zeros((16, 128), jnp.float32)
    old[pl.ds(0, 16), :] = zeros
    old[pl.ds(1040, 16), :] = zeros
    for k in range(CHUNKS):
        recv[k][pl.ds(0, 8), :] = zeros[:8]
        recv[k][pl.ds(8 + 64 * SLOT[k], 8), :] = zeros[:8]

    lane = lax.broadcasted_iota(jnp.int32, (8, 128), 1)
    upper = lax.broadcasted_iota(jnp.int32, (8, 128), 0) < 4
    loads[0].wait()

    def leaving(i, c):
        first, last = c
        hit = lane == new_owner[i]
        return jnp.where(hit & (first < 0), i, first), jnp.where(hit, i, last)

    none = jnp.full((8, 128), -1, jnp.int32)
    first, last = lax.fori_loop(0, 64, leaving, (none, none), unroll=8)
    index_v[0] = jnp.maximum(first, 0) * 16
    index_v[1] = jnp.maximum(last, 0) * 16
    to_s = pltpu.make_async_copy(index_v.at[pl.ds(0, 2)], index_s.at[pl.ds(0, 2)], index_sem.at[0])
    to_s.start()
    loads[2].wait()
    to_s.wait()

    def pack(r, c):
        px = ((cy + (r // 8) % 4) % 4) * 2 + (core + r // 32) % 2
        owner = px * 8 + (gz + r) % 8
        a, b = index_s[0, 0, owner], index_s[1, 0, owner]
        for f in range(F):
            va = old[pl.ds(16 + a + f, 8, stride=4), :]
            vb = old[pl.ds(b + f, 8, stride=4), :]
            k = next(k for k in range(CHUNKS) if f in FIELDS[k])
            row = pl.multiple_of(r * SLOT[k] + FIELDS[k].index(f) * 8, 8)
            send[k][pl.ds(row, 8), :] = jnp.where(upper, va, vb)
        return c

    lax.fori_loop(0, 64, pack, 0, unroll=4)
    for k in range(CHUNKS):
        recv[k][pl.ds(8, SLOT[k]), :] = send[k][pl.ds(0, SLOT[k]), :]

    def post(k, near, far):
        for c, y, z in OTHERS:
            if not near < hops(c, y, z) <= far:
                continue
            pltpu.make_async_remote_copy(
                src_ref=send[k].at[pl.ds(number(c, y, z) * SLOT[k], SLOT[k])],
                dst_ref=recv[k].at[pl.ds(8 + number(c, -y, -z) * SLOT[k], SLOT[k])],
                send_sem=send_sem.at[k],
                recv_sem=recv_sem.at[k],
                device_id=peer(c, y, z),
                device_id_type=MESH,
            ).start()

    last = len(KNOWN) - 1
    for r, far in enumerate(KNOWN):
        if r:
            pl.semaphore_wait(ready.at[r - 1], len(ball(GREET[r])))
        else:
            pl.semaphore_wait(barrier, len(ball(GREET[0])) + 2)
        if r < last:
            greet(ready.at[r], r + 1)
        post(0, KNOWN[r - 1] if r else 0, far)
        if r == 0:
            post(1, 0, 2)
    post(1, 2, 7)

    loads[1].wait()

    def owners(i, c):
        return jnp.where(lane == i, old_owner[i], c)

    owner = lax.fori_loop(0, 64, owners, none, unroll=8)

    def ranks(i, c):
        return jnp.where((lane > i) & (owner == old_owner[i]), 4, c)

    rank = lax.fori_loop(0, 64, ranks, jnp.zeros((8, 128), jnp.int32), unroll=8)
    ox, oz = owner // 8, owner % 8
    slot = ((ox % 2 - core + 2) % 2 * 4 + (ox // 2 - cy + 4) % 4) * 8 + (oz - gz + 8) % 8
    for k in range(CHUNKS):
        index_v[2 + k] = slot * SLOT[k] + rank
    to_s = pltpu.make_async_copy(
        index_v.at[pl.ds(2, CHUNKS)], index_s.at[pl.ds(2, CHUNKS)], index_sem.at[1]
    )
    to_s.start()
    to_s.wait()

    def arrived(k):
        everyone = recv[k].at[pl.ds(8 + SLOT[k], 63 * SLOT[k])]
        pltpu.make_async_copy(everyone, everyone, recv_sem.at[k]).wait()

    bits = [((lane // 8) & step) != 0 for step in (1, 2, 4, 8)]

    def reorder(k):
        def one(s, c):
            f, by = s // 2, s % 2
            v = []
            for bz in range(16):
                a = index_s[2 + k, 0, by * 16 + bz] + f * 8
                b = index_s[2 + k, 0, by * 16 + bz + 32] + f * 8
                box = jnp.where(upper, recv[k][pl.ds(8 + a, 8), :], recv[k][pl.ds(4 + b, 8), :])
                v.append(pltpu.roll(box, 8 * bz, 1) if bz else box)
            for n, bit in enumerate(bits):
                v = [jnp.where(bit, v[(i + (1 << n)) % 16], v[i]) for i in range(16)]
            for g in range(16):
                start = (g // 8 + 1) * STRIDE + 8 + by * 8 + g % 8
                value = pltpu.roll(v[16 - g], 128 - 8 * g, 1) if g else v[0]
                grid0[FIELDS[k][0] + f, pl.ds(start, 8, stride=2 * STRIDE), :] = value
            return c

        lax.fori_loop(0, 2 * len(FIELDS[k]), one, 0, unroll=2)

    def rows(x, y=0):
        if y:
            return pl.ds((x + 1) * STRIDE + 8 + y, EDGE)
        return pl.ds(pl.multiple_of((x + 1) * STRIDE + 8, 8), EDGE)

    def pack_z(x, f, v, ends):
        ends = list(ends)
        for half in range(2):
            twice = (f % 2) * 64 + x * 4 + half * 2
            here = ((lane + 1 - twice) & 127) < 2
            ends[f // 2] = jnp.where(here, pltpu.roll(v[half * 8 : half * 8 + 8], twice, 1), ends[f // 2])
        return tuple(ends)

    def exchange(s, k, ends):
        grid = grids[s]
        fields = pl.ds(FIELDS[k][0], len(FIELDS[k]))
        copies = []

        def send_face(n, side, axis, here, size, source, target):
            copy = pltpu.make_async_remote_copy(
                src_ref=source,
                dst_ref=target,
                send_sem=face_send.at[s, k, n, side],
                recv_sem=face_recv.at[s, k, n, 1 - side],
                device_id={axis: (here + (1 if side else size - 1)) % size},
                device_id_type=MESH,
            )
            copy.start()
            copies.append(copy)

        for side in range(2):
            source = grid.at[fields, pl.ds(STRIDE * (16 if side else 1) + 8, EDGE)]
            target = grid.at[fields, pl.ds(STRIDE * (0 if side else 17) + 8, EDGE)]
            send_face(2, side, "gx", gx, 8, source, target)
        for side in range(2):
            for f, field in enumerate(FIELDS[k]):
                for part in range(2):
                    fy[k][s, side, pl.ds(f * 16 + part * 8, 8)] = grid[
                        field, pl.ds((part * 8 + 1) * STRIDE + 8 + side * 15, 8, stride=STRIDE), :
                    ]
            send_face(1, side, "gy", gy, 4, fy[k].at[s, side], hy[k].at[s, 1 - side])
        if callable(ends):
            ends = ends()
        for n, value in enumerate(ends):
            fz[k][s, pl.ds(n * 8, 8)] = value
        for side in range(2):
            send_face(0, side, "gz", gz, 8, fz[k].at[s], hz[k].at[s, 1 - side])
        everything.extend(copies)
        return copies

    odd = lane % 2 == 1

    def receive(s, k, copies):
        for copy in copies:
            copy.wait_recv()
        for side in range(2):
            for f, field in enumerate(FIELDS[k]):
                for part in range(2):
                    start = (part * 8 + 1) * STRIDE + (24 if side else 7)
                    grids[s][field, pl.ds(start, 8, stride=STRIDE), :] = hy[k][
                        s, side, pl.ds(f * 16 + part * 8, 8)
                    ]
        return [
            jnp.where(odd, hz[k][s, 0, pl.ds(n * 8, 8)], pltpu.roll(hz[k][s, 1, pl.ds(n * 8, 8)], 126, 1))
            for n in range(PARTS[k])
        ]

    wide = lax.broadcasted_iota(jnp.int32, (16, 128), 1)

    def beside_z(v, edges, x, f):
        twice = (f % 2) * 64 + x * 4
        edge = jnp.concatenate([pltpu.roll(edges[f // 2], (129 - twice - 2 * h) % 128, 1) for h in range(2)], 0)
        return (
            jnp.where(wide == 0, edge, pltpu.roll(v, 1, 1)),
            jnp.where(wide == 127, edge, pltpu.roll(v, 127, 1)),
        )

    def coefficients(s, edges):
        grid = grids[s]

        def diffusivity(x, c):
            part = pl.ds(pl.multiple_of(x * STRIDE, 8), STRIDE)
            diff[part, :] = coefficient(grid[0, part, :])
            return c

        lax.fori_loop(0, 18, diffusivity, 0, unroll=3)
        edges = [coefficient(edge) for edge in edges]

        def plane(x, c):
            d = diff[rows(x), :]
            near = (diff[rows(x - 1), :], diff[rows(x + 1), :], diff[rows(x, -1), :], diff[rows(x, 1), :])
            for n, value in enumerate(near + beside_z(d, edges, x, 0)):
                coef[s, n, pl.ds(pl.multiple_of(x * EDGE, EDGE), EDGE), :] = (0.5 * TIME_STEP) * (d + value)
            return c

        lax.fori_loop(0, 16, plane, 0, unroll=UNROLL)

    def section(s, k, copies, emit, start):
        grid = grids[s]
        edges = receive(s, k, copies)
        if k == 0:
            coefficients(s, edges)

        def plane(x, c):
            faces = [coef[s, n, pl.ds(pl.multiple_of(x * EDGE, EDGE), EDGE), :] for n in range(6)]
            for f, field in enumerate(FIELDS[k]):
                v = grid[field, rows(x), :]
                near = (
                    grid[field, rows(x - 1), :],
                    grid[field, rows(x + 1), :],
                    grid[field, rows(x, -1), :],
                    grid[field, rows(x, 1), :],
                ) + beside_z(v, edges, x, f)
                total = faces[0] * (near[0] - v)
                for a, n in zip(faces[1:], near[1:]):
                    total = total + a * (n - v)
                c = emit(x, f, field, v, DIFFUSION[field] * total, c)
            return c

        return lax.fori_loop(0, 16, plane, start, unroll=16 if k else UNROLL)

    nothing = [(jnp.zeros((8, 128), jnp.float32),) * PARTS[k] for k in range(CHUNKS)]
    everything = []

    def to_grid(k):
        arrived(k)
        reorder(k)

        def first_ends(x, ends):
            for f, field in enumerate(FIELDS[k]):
                ends = pack_z(x, f, grid0[field, rows(x), :], ends)
            return ends

        return exchange(0, k, lambda: lax.fori_loop(0, 16, first_ends, nothing[k], unroll=16 if k else 4))

    def first_section(k, copies):
        def keep(x, f, field, v, change, ends):
            w = v + change
            grid1[field, rows(x), :] = w
            return pack_z(x, f, w, ends)

        return exchange(1, k, section(0, k, copies, keep, nothing[k]))

    def second_section(k, copies):
        def finish(x, f, field, w, change, c):
            out[field, x] = 0.5 * grid0[field, rows(x), :] + 0.5 * (w + change)
            return c

        section(1, k, copies, finish, 0)

    def settle():
        for copy in everything[: len(everything) - 6]:
            copy.wait_send()
        for k in range(CHUNKS):
            sent = send[k].at[pl.ds(SLOT[k], 63 * SLOT[k])]
            pltpu.make_async_copy(sent, sent, send_sem.at[k]).wait()

    faces = [to_grid(k) for k in range(CHUNKS)]
    faces = [first_section(k, faces[k]) for k in range(CHUNKS)]
    for k in range(CHUNKS - 1):
        second_section(k, faces[k])
    settle()
    second_section(CHUNKS - 1, faces[-1])
    for copy in everything[-6:]:
        copy.wait_send()


def body(old_fields, new_owner, old_owner):
    boxes = old_fields.reshape(64, 4, 4, 128).transpose(0, 2, 1, 3).reshape(1024, 128)
    f32 = jnp.float32
    operands = [pltpu.with_memory_space_constraint(v, pltpu.HBM) for v in (boxes, new_owner, old_owner)]
    return pl.pallas_call(
        kernel,
        out_shape=jax.ShapeDtypeStruct((F, EDGE, EDGE, 128), f32),
        in_specs=[pl.BlockSpec(memory_space=pltpu.HBM)] * 3,
        out_specs=pl.BlockSpec(memory_space=pltpu.VMEM),
        scratch_shapes=[
            pltpu.VMEM((1056, 128), f32),
            [pltpu.VMEM((64 * rows, 128), f32) for rows in SLOT],
            [pltpu.VMEM((64 * rows + 16, 128), f32) for rows in SLOT],
            pltpu.VMEM((F, GRID, 128), f32),
            pltpu.VMEM((F, GRID, 128), f32),
            pltpu.VMEM((EDGE * STRIDE + 3 * STRIDE, 128), f32),
            pltpu.VMEM((2, 6, EDGE * EDGE, 128), f32),
            [pltpu.VMEM((2, 2, rows * 2, 128), f32) for rows in SLOT],
            [pltpu.VMEM((2, parts * 8, 128), f32) for parts in PARTS],
            [pltpu.VMEM((2, 2, rows * 2, 128), f32) for rows in SLOT],
            [pltpu.VMEM((2, 2, parts * 8, 128), f32) for parts in PARTS],
            pltpu.VMEM((2 + CHUNKS, 8, 128), jnp.int32),
            pltpu.SMEM((2 + CHUNKS, 8, 128), jnp.int32),
            pltpu.SMEM((64,), jnp.int32),
            pltpu.SMEM((64,), jnp.int32),
            pltpu.SemaphoreType.DMA,
            pltpu.SemaphoreType.DMA((2,)),
            pltpu.SemaphoreType.DMA((2,)),
            pltpu.SemaphoreType.REGULAR((len(KNOWN),)),
            pltpu.SemaphoreType.DMA((CHUNKS,)),
            pltpu.SemaphoreType.DMA((CHUNKS,)),
            pltpu.SemaphoreType.DMA((2, CHUNKS, 3, 2)),
            pltpu.SemaphoreType.DMA((2, CHUNKS, 3, 2)),
        ],
        compiler_params=pltpu.CompilerParams(
            collective_id=0, has_side_effects=True, vmem_limit_bytes=32 * 2**20
        ),
        name="move_and_diffuse",
    )(*operands)


def solution(mesh):
    return jax.shard_map(
        body,
        mesh=mesh,
        in_specs=(P(("gx", "gy", "gz"), None, None), P(("gx", "gy", "gz")), P(("gx", "gy", "gz"))),
        out_specs=P(None, "gx", "gy", "gz"),
        check_vma=False,
    )
```

```python
import jax
import jax.numpy as jnp
from jax import lax
from jax.experimental import pallas as pl
from jax.experimental.pallas import tpu as pltpu
from jax.sharding import PartitionSpec as P

DIFFUSION = (1.0, 3.3, 0.9, 1.2)
TIME_STEP = 0.012
MESH = pl.DeviceIdType.MESH
F = 4
FIELDS = ((0, 1, 2), (3,))
CHUNKS = len(FIELDS)
SLOT = [8 * len(fields) for fields in FIELDS]
PARTS = [(len(fields) + 1) // 2 for fields in FIELDS]
UNROLL = 8
EDGE = 16
STRIDE = 24
GRID = (EDGE + 2) * STRIDE + 8

OTHERS = sorted(
    [(c, y, z) for c in range(2) for y in range(4) for z in range(8) if c or y or z],
    key=lambda d: -d[0] - min(d[1], 4 - d[1]) - min(d[2], 8 - d[2]),
)


def hops(c, y, z):
    return c + min(y, 4 - y) + min(z, 8 - z)


def ball(n):
    return [d for d in OTHERS if hops(*d) <= n]


GREET = (2, 2, 3)
KNOWN = (2, 4, 7)


def number(c, y, z):
    return (c * 4 + y % 4) * 8 + z % 8


def coefficient(t):
    return t * jnp.sqrt(t)


def kernel(
    old_hbm, new_hbm, own_hbm, out,
    old, send, recv, grid0, grid1, diff, coef, fy, fz, hy, hz, index_v, index_s, new_owner, old_owner,
    old_sem, owner_sem, index_sem, ready, send_sem, recv_sem, face_send, face_recv,
):
    gx, gy, gz = lax.axis_index("gx"), lax.axis_index("gy"), lax.axis_index("gz")
    core, cy = gx % 2, gx // 2
    grids = (grid0, grid1)

    def peer(c, y, z):
        where = {}
        if c or y:
            where["gx"] = ((cy + y) % 4) * 2 + (core + c) % 2
        if z:
            where["gz"] = (gz + z) % 8
        return where

    barrier = pltpu.get_barrier_semaphore()
    def greet(sem, r):
        for d in ball(GREET[r]):
            pl.semaphore_signal(sem, inc=1, device_id=peer(*d), device_id_type=MESH)

    greet(barrier, 0)
    for y in (1, 3):
        pl.semaphore_signal(barrier, inc=1, device_id={"gy": (gy + y) % 4}, device_id_type=MESH)
    loads = [
        pltpu.make_async_copy(new_hbm, new_owner, owner_sem.at[0]),
        pltpu.make_async_copy(own_hbm, old_owner, owner_sem.at[1]),
        pltpu.make_async_copy(old_hbm, old.at[pl.ds(16, 1024)], old_sem),
    ]
    for load in loads:
        load.start()
    zeros = jnp.zeros((16, 128), jnp.float32)
    old[pl.ds(0, 16), :] = zeros
    old[pl.ds(1040, 16), :] = zeros
    for k in range(CHUNKS):
        recv[k][pl.ds(0, 8), :] = zeros[:8]
        recv[k][pl.ds(8 + 64 * SLOT[k], 8), :] = zeros[:8]

    lane = lax.broadcasted_iota(jnp.int32, (8, 128), 1)
    upper = lax.broadcasted_iota(jnp.int32, (8, 128), 0) < 4
    loads[0].wait()

    def leaving(i, c):
        first, last = c
        hit = lane == new_owner[i]
        return jnp.where(hit & (first < 0), i, first), jnp.where(hit, i, last)

    none = jnp.full((8, 128), -1, jnp.int32)
    first, last = lax.fori_loop(0, 64, leaving, (none, none), unroll=8)
    index_v[0] = jnp.maximum(first, 0) * 16
    index_v[1] = jnp.maximum(last, 0) * 16
    to_s = pltpu.make_async_copy(index_v.at[pl.ds(0, 2)], index_s.at[pl.ds(0, 2)], index_sem.at[0])
    to_s.start()
    loads[2].wait()
    to_s.wait()

    def pack(r, c):
        px = ((cy + (r // 8) % 4) % 4) * 2 + (core + r // 32) % 2
        owner = px * 8 + (gz + r) % 8
        a, b = index_s[0, 0, owner], index_s[1, 0, owner]
        for f in range(F):
            va = old[pl.ds(16 + a + f, 8, stride=4), :]
            vb = old[pl.ds(b + f, 8, stride=4), :]
            k = next(k for k in range(CHUNKS) if f in FIELDS[k])
            row = pl.multiple_of(r * SLOT[k] + FIELDS[k].index(f) * 8, 8)
            send[k][pl.ds(row, 8), :] = jnp.where(upper, va, vb)
        return c

    lax.fori_loop(0, 64, pack, 0, unroll=4)
    for k in range(CHUNKS):
        recv[k][pl.ds(8, SLOT[k]), :] = send[k][pl.ds(0, SLOT[k]), :]

    def post(k, near, far):
        for c, y, z in OTHERS:
            if not near < hops(c, y, z) <= far:
                continue
            pltpu.make_async_remote_copy(
                src_ref=send[k].at[pl.ds(number(c, y, z) * SLOT[k], SLOT[k])],
                dst_ref=recv[k].at[pl.ds(8 + number(c, -y, -z) * SLOT[k], SLOT[k])],
                send_sem=send_sem.at[k],
                recv_sem=recv_sem.at[k],
                device_id=peer(c, y, z),
                device_id_type=MESH,
            ).start()

    last = len(KNOWN) - 1
    for r, far in enumerate(KNOWN):
        if r:
            pl.semaphore_wait(ready.at[r - 1], len(ball(GREET[r])))
        else:
            pl.semaphore_wait(barrier, len(ball(GREET[0])) + 2)
        if r < last:
            greet(ready.at[r], r + 1)
        post(0, KNOWN[r - 1] if r else 0, far)
        if r == 0:
            post(1, 0, 2)
    post(1, 2, 7)

    loads[1].wait()

    def owners(i, c):
        return jnp.where(lane == i, old_owner[i], c)

    owner = lax.fori_loop(0, 64, owners, none, unroll=8)

    def ranks(i, c):
        return jnp.where((lane > i) & (owner == old_owner[i]), 4, c)

    rank = lax.fori_loop(0, 64, ranks, jnp.zeros((8, 128), jnp.int32), unroll=8)
    ox, oz = owner // 8, owner % 8
    slot = ((ox % 2 - core + 2) % 2 * 4 + (ox // 2 - cy + 4) % 4) * 8 + (oz - gz + 8) % 8
    for k in range(CHUNKS):
        index_v[2 + k] = slot * SLOT[k] + rank
    to_s = pltpu.make_async_copy(
        index_v.at[pl.ds(2, CHUNKS)], index_s.at[pl.ds(2, CHUNKS)], index_sem.at[1]
    )
    to_s.start()
    to_s.wait()

    def arrived(k):
        everyone = recv[k].at[pl.ds(8 + SLOT[k], 63 * SLOT[k])]
        pltpu.make_async_copy(everyone, everyone, recv_sem.at[k]).wait()

    bits = [((lane // 8) & step) != 0 for step in (1, 2, 4, 8)]

    def reorder(k):
        def one(s, c):
            f, by = s // 2, s % 2
            v = []
            for bz in range(16):
                a = index_s[2 + k, 0, by * 16 + bz] + f * 8
                b = index_s[2 + k, 0, by * 16 + bz + 32] + f * 8
                box = jnp.where(upper, recv[k][pl.ds(8 + a, 8), :], recv[k][pl.ds(4 + b, 8), :])
                v.append(pltpu.roll(box, 8 * bz, 1) if bz else box)
            for n, bit in enumerate(bits):
                v = [jnp.where(bit, v[(i + (1 << n)) % 16], v[i]) for i in range(16)]
            for g in range(16):
                start = (g // 8 + 1) * STRIDE + 8 + by * 8 + g % 8
                value = pltpu.roll(v[16 - g], 128 - 8 * g, 1) if g else v[0]
                grid0[FIELDS[k][0] + f, pl.ds(start, 8, stride=2 * STRIDE), :] = value
            return c

        lax.fori_loop(0, 2 * len(FIELDS[k]), one, 0, unroll=2)

    def rows(x, y=0):
        if y:
            return pl.ds((x + 1) * STRIDE + 8 + y, EDGE)
        return pl.ds(pl.multiple_of((x + 1) * STRIDE + 8, 8), EDGE)

    def pack_z(x, f, v, ends):
        ends = list(ends)
        for half in range(2):
            twice = (f % 2) * 64 + x * 4 + half * 2
            here = ((lane + 1 - twice) & 127) < 2
            ends[f // 2] = jnp.where(here, pltpu.roll(v[half * 8 : half * 8 + 8], twice, 1), ends[f // 2])
        return tuple(ends)

    def exchange(s, k, ends):
        grid = grids[s]
        fields = pl.ds(FIELDS[k][0], len(FIELDS[k]))
        copies = []

        def send_face(n, side, axis, here, size, source, target):
            copy = pltpu.make_async_remote_copy(
                src_ref=source,
                dst_ref=target,
                send_sem=face_send.at[s, k, n, side],
                recv_sem=face_recv.at[s, k, n, 1 - side],
                device_id={axis: (here + (1 if side else size - 1)) % size},
                device_id_type=MESH,
            )
            copy.start()
            copies.append(copy)

        for side in range(2):
            source = grid.at[fields, pl.ds(STRIDE * (16 if side else 1) + 8, EDGE)]
            target = grid.at[fields, pl.ds(STRIDE * (0 if side else 17) + 8, EDGE)]
            send_face(2, side, "gx", gx, 8, source, target)
        for side in range(2):
            for f, field in enumerate(FIELDS[k]):
                for part in range(2):
                    fy[k][s, side, pl.ds(f * 16 + part * 8, 8)] = grid[
                        field, pl.ds((part * 8 + 1) * STRIDE + 8 + side * 15, 8, stride=STRIDE), :
                    ]
            send_face(1, side, "gy", gy, 4, fy[k].at[s, side], hy[k].at[s, 1 - side])
        if callable(ends):
            ends = ends()
        for n, value in enumerate(ends):
            fz[k][s, pl.ds(n * 8, 8)] = value
        for side in range(2):
            send_face(0, side, "gz", gz, 8, fz[k].at[s], hz[k].at[s, 1 - side])
        everything.extend(copies)
        return copies

    odd = lane % 2 == 1

    def receive(s, k, copies):
        for copy in copies:
            copy.wait_recv()
        for side in range(2):
            for f, field in enumerate(FIELDS[k]):
                for part in range(2):
                    start = (part * 8 + 1) * STRIDE + (24 if side else 7)
                    grids[s][field, pl.ds(start, 8, stride=STRIDE), :] = hy[k][
                        s, side, pl.ds(f * 16 + part * 8, 8)
                    ]
        return [
            jnp.where(odd, hz[k][s, 0, pl.ds(n * 8, 8)], pltpu.roll(hz[k][s, 1, pl.ds(n * 8, 8)], 126, 1))
            for n in range(PARTS[k])
        ]

    wide = lax.broadcasted_iota(jnp.int32, (16, 128), 1)

    def beside_z(v, edges, x, f):
        twice = (f % 2) * 64 + x * 4
        edge = jnp.concatenate([pltpu.roll(edges[f // 2], (129 - twice - 2 * h) % 128, 1) for h in range(2)], 0)
        return (
            jnp.where(wide == 0, edge, pltpu.roll(v, 1, 1)),
            jnp.where(wide == 127, edge, pltpu.roll(v, 127, 1)),
        )

    def coefficients(s, edges):
        grid = grids[s]

        def diffusivity(x, c):
            part = pl.ds(pl.multiple_of(x * STRIDE, 8), STRIDE)
            diff[part, :] = coefficient(grid[0, part, :])
            return c

        lax.fori_loop(0, 18, diffusivity, 0, unroll=6)
        edges = [coefficient(edge) for edge in edges]

        def plane(x, c):
            d = diff[rows(x), :]
            near = (diff[rows(x - 1), :], diff[rows(x + 1), :], diff[rows(x, -1), :], diff[rows(x, 1), :])
            for n, value in enumerate(near + beside_z(d, edges, x, 0)):
                coef[s, n, pl.ds(pl.multiple_of(x * EDGE, EDGE), EDGE), :] = (0.5 * TIME_STEP) * (d + value)
            return c

        lax.fori_loop(0, 16, plane, 0, unroll=16)

    def section(s, k, copies, emit, start):
        grid = grids[s]
        edges = receive(s, k, copies)
        if k == 0:
            coefficients(s, edges)

        def plane(x, c):
            faces = [coef[s, n, pl.ds(pl.multiple_of(x * EDGE, EDGE), EDGE), :] for n in range(6)]
            for f, field in enumerate(FIELDS[k]):
                v = grid[field, rows(x), :]
                near = (
                    grid[field, rows(x - 1), :],
                    grid[field, rows(x + 1), :],
                    grid[field, rows(x, -1), :],
                    grid[field, rows(x, 1), :],
                ) + beside_z(v, edges, x, f)
                total = faces[0] * (near[0] - v)
                for a, n in zip(faces[1:], near[1:]):
                    total = total + a * (n - v)
                c = emit(x, f, field, v, DIFFUSION[field] * total, c)
            return c

        return lax.fori_loop(0, 16, plane, start, unroll=16 if k else UNROLL)

    nothing = [(jnp.zeros((8, 128), jnp.float32),) * PARTS[k] for k in range(CHUNKS)]
    everything = []

    def to_grid(k):
        arrived(k)
        reorder(k)

        def first_ends(x, ends):
            for f, field in enumerate(FIELDS[k]):
                ends = pack_z(x, f, grid0[field, rows(x), :], ends)
            return ends

        return exchange(0, k, lambda: lax.fori_loop(0, 16, first_ends, nothing[k], unroll=16 if k else 4))

    def first_section(k, copies):
        def keep(x, f, field, v, change, ends):
            w = v + change
            grid1[field, rows(x), :] = w
            return pack_z(x, f, w, ends)

        return exchange(1, k, section(0, k, copies, keep, nothing[k]))

    def second_section(k, copies):
        def finish(x, f, field, w, change, c):
            out[field, x] = 0.5 * grid0[field, rows(x), :] + 0.5 * (w + change)
            return c

        section(1, k, copies, finish, 0)

    def settle():
        for copy in everything[: len(everything) - 6]:
            copy.wait_send()
        for k in range(CHUNKS):
            sent = send[k].at[pl.ds(SLOT[k], 63 * SLOT[k])]
            pltpu.make_async_copy(sent, sent, send_sem.at[k]).wait()

    faces = [to_grid(k) for k in range(CHUNKS)]
    faces = [first_section(k, faces[k]) for k in range(CHUNKS)]
    for k in range(CHUNKS - 1):
        second_section(k, faces[k])
    settle()
    second_section(CHUNKS - 1, faces[-1])
    for copy in everything[-6:]:
        copy.wait_send()


def body(old_fields, new_owner, old_owner):
    boxes = old_fields.reshape(64, 4, 4, 128).transpose(0, 2, 1, 3).reshape(1024, 128)
    f32 = jnp.float32
    operands = [pltpu.with_memory_space_constraint(v, pltpu.HBM) for v in (boxes, new_owner, old_owner)]
    return pl.pallas_call(
        kernel,
        out_shape=jax.ShapeDtypeStruct((F, EDGE, EDGE, 128), f32),
        in_specs=[pl.BlockSpec(memory_space=pltpu.HBM)] * 3,
        out_specs=pl.BlockSpec(memory_space=pltpu.VMEM),
        scratch_shapes=[
            pltpu.VMEM((1056, 128), f32),
            [pltpu.VMEM((64 * rows, 128), f32) for rows in SLOT],
            [pltpu.VMEM((64 * rows + 16, 128), f32) for rows in SLOT],
            pltpu.VMEM((F, GRID, 128), f32),
            pltpu.VMEM((F, GRID, 128), f32),
            pltpu.VMEM((EDGE * STRIDE + 3 * STRIDE, 128), f32),
            pltpu.VMEM((2, 6, EDGE * EDGE, 128), f32),
            [pltpu.VMEM((2, 2, rows * 2, 128), f32) for rows in SLOT],
            [pltpu.VMEM((2, parts * 8, 128), f32) for parts in PARTS],
            [pltpu.VMEM((2, 2, rows * 2, 128), f32) for rows in SLOT],
            [pltpu.VMEM((2, 2, parts * 8, 128), f32) for parts in PARTS],
            pltpu.VMEM((2 + CHUNKS, 8, 128), jnp.int32),
            pltpu.SMEM((2 + CHUNKS, 8, 128), jnp.int32),
            pltpu.SMEM((64,), jnp.int32),
            pltpu.SMEM((64,), jnp.int32),
            pltpu.SemaphoreType.DMA,
            pltpu.SemaphoreType.DMA((2,)),
            pltpu.SemaphoreType.DMA((2,)),
            pltpu.SemaphoreType.REGULAR((len(KNOWN),)),
            pltpu.SemaphoreType.DMA((CHUNKS,)),
            pltpu.SemaphoreType.DMA((CHUNKS,)),
            pltpu.SemaphoreType.DMA((2, CHUNKS, 3, 2)),
            pltpu.SemaphoreType.DMA((2, CHUNKS, 3, 2)),
        ],
        compiler_params=pltpu.CompilerParams(
            collective_id=0, has_side_effects=True, vmem_limit_bytes=32 * 2**20
        ),
        name="move_and_diffuse",
    )(*operands)


def solution(mesh):
    return jax.shard_map(
        body,
        mesh=mesh,
        in_specs=(P(("gx", "gy", "gz"), None, None), P(("gx", "gy", "gz")), P(("gx", "gy", "gz"))),
        out_specs=P(None, "gx", "gy", "gz"),
        check_vma=False,
    )
```
